256 devices in a mesh: team: 2 (over y_hi), gx: 8 (over x, core), gy: 16 (over z, y_lo).
Axes of the slice: x: 4, y: 4 (y_hi: 2, y_lo: 2; y = y_hi * 2 + y_lo), z: 8, core: 2. Of those that a mesh axis runs over, the one named last changes fastest.
Arguments:
- state: float32 [2, 256, 256, 128], P('team', 'gx', 'gy'), may hold values from -6 to 6
- coef: float32 [2, 256, 256, 128], P('team', 'gx', 'gy'), may hold values from 0.5 to 2
- mask: int32 [256, 256, 16], P('gx', 'gy'), may hold values 0 or 1
- src_brick: int32 [8, 16], replicated, may hold values from 0 to 16383
- power: float32 [8, 16], replicated, may hold values from 1 to 4
Outputs:
- final_state: float32 [2, 256, 256, 128], P('team', 'gx', 'gy')
The draws below stay inside these ranges and needn't reach their ends.
All inputs are finite; a program needn't handle non-finite values. No bound on the sum of `mask` on one device may be relied on, other than what follows from the above.
Results may differ from the reference program's by a relative error of at most 0.00007.
Values sent between devices are 32-bit elements; how exact they have to be, the bound alone decides.
A program may use at most 64 MiB of HBM per device.

```python
import math
import jax
import jax.numpy as jnp

NZ = 128
BRICK = 8
NSRC = 16
MACRO = 2
SUBS = 4
NX = 256
NY = 256
NBRICK = 16384


def set_ends(array, stream_key, smallest, top_value):
    spot = [jax.random.randint(jax.random.fold_in(stream_key, axis), (), 0, length) for axis, length in enumerate(array.shape)]
    widest = array.shape.index(max(array.shape))
    beside = spot[:widest] + [(spot[widest] + 1) % array.shape[widest]] + spot[widest + 1:]
    return array.at[tuple(spot)].set(smallest).at[tuple(beside)].set(top_value)


def block_levels(rng, extent, split, least, largest):
    loudness = 1.0
    for position, blocks in split:
        steps = jax.random.uniform(jax.random.fold_in(jax.random.fold_in(rng, 6), position), (blocks,), jnp.float32, least / len(split), largest / len(split))
        loudness = loudness * jnp.repeat(jnp.exp(steps), extent[position] // blocks).reshape((-1,) + (1,) * (len(extent) - 1 - position))
    return loudness


def centred(stream_key, extent, deviation, limit, pieces=(), kind=jnp.bfloat16):
    factor_of = block_levels(stream_key, extent, pieces, -0.22, 0.18) if pieces else 1.0
    values = jax.random.normal(stream_key, extent, jnp.float32) * deviation * factor_of
    return jnp.minimum(jnp.maximum(values, -limit), limit).astype(kind)


def setup_inputs(seed: int = 0) -> dict:
    key_list = jax.random.split(jax.random.key(seed), 6)
    state = centred(key_list[0], (2, NX, NY, NZ), 1.0, 6.0, ((0, 2), (1, 8), (2, 16)), jnp.float32)
    coef = jnp.clip(jnp.exp(math.log(2.0) - 1.3862944 * jax.random.uniform(key_list[1], (2, NX, NY, NZ), jnp.float32) ** block_levels(key_list[1], (2, NX, NY, NZ), ((0, 2), (1, 8), (2, 16)), -0.2, 0.2)), 0.5, 2.0)
    mask = set_ends((jax.random.randint(key_list[2], (NX, NY, NZ // BRICK), 0, 4) < 3).astype(jnp.int32), jax.random.fold_in(key_list[2], 1), 0, 1)
    src_brick = set_ends(jax.random.randint(key_list[3], (MACRO * SUBS, NSRC), 0, NBRICK), jax.random.fold_in(key_list[3], 1), 0, NBRICK - 1).astype(jnp.int32)
    power = jnp.clip(jnp.exp(jax.random.uniform(key_list[4], (MACRO * SUBS, NSRC), jnp.float32, math.log(1.0), math.log(4.0))), 1.0, 4.0)
    return {"state": state, "coef": coef, "mask": mask, "src_brick": src_brick, "power": power}


def face_table():
    result = []
    for axis_pos in range(3):
        for sign in (-1, 1):
            offset = [0, 0, 0]
            offset[axis_pos] = sign
            result.append((offset[0], offset[1], offset[2], 1.0))
    return result


def solid_table():
    result = []
    for first in (-1, 0, 1):
        for second in (-1, 0, 1):
            for third in (-1, 0, 1):
                nonzero = abs(first) + abs(second) + abs(third)
                if nonzero == 2:
                    result.append((first, second, third, 1.0 / 6.0))
                if nonzero == 3:
                    result.append((first, second, third, 1.0 / 12.0))
    return result


def flow_terms(field, coupled, table):
    padded_u = jnp.pad(field, 1)
    padded_k = jnp.pad(coupled, 1)
    sizes = field.shape
    balance = jnp.zeros(sizes, jnp.float32)
    weights = jnp.zeros(sizes, jnp.float32)
    for first, second, third, factor in table:
        near_u = padded_u[1 + first:1 + first + sizes[0], 1 + second:1 + second + sizes[1], 1 + third:1 + third + sizes[2]]
        near_k = padded_k[1 + first:1 + first + sizes[0], 1 + second:1 + second + sizes[1], 1 + third:1 + third + sizes[2]]
        conduct = factor * 0.5 * (coupled + near_k)
        balance = balance + conduct * (near_u - field)
        weights = weights + conduct
    return balance, weights


def shift_down(field):
    return jnp.concatenate([field[:, :, 1:], jnp.zeros_like(field[:, :, :1])], axis=2)


def shift_up(field):
    return jnp.concatenate([jnp.zeros_like(field[:, :, :1]), field[:, :, :-1]], axis=2)


def plastic(disp):
    slope = shift_down(disp) - disp
    return 0.5 * slope * slope


def source_field(bricks, powers):
    nxb = NX // BRICK
    nyb = NY // BRICK
    nzb = NZ // BRICK
    flat = jnp.zeros((nxb * nyb * nzb,), jnp.float32).at[bricks].add(powers)
    grid = flat.reshape(nxb, nyb, nzb)
    grid = jnp.repeat(grid, BRICK, axis=0)
    grid = jnp.repeat(grid, BRICK, axis=1)
    return jnp.repeat(grid, BRICK, axis=2)


def reference(state, coef, mask, src_brick, power):
    temp = state[0]
    disp = state[1]
    active = jnp.repeat(jnp.where(mask == 1, 1.0, 0.05).astype(jnp.float32), BRICK, axis=2)
    base_t = coef[0] * active
    base_m = coef[1] * active
    lagged = temp
    heat = plastic(disp)
    faces = face_table()
    solid = solid_table()
    for macro in range(MACRO):
        for substep in range(SUBS):
            index = macro * SUBS + substep
            cond_k = base_t * (1.0 + 0.5 * jnp.tanh(temp))
            balance, unused = flow_terms(temp, cond_k, faces)
            temp = temp + 0.05 * (balance + source_field(src_brick[index], power[index]) + heat)
            slope = shift_down(disp) - disp
            stiff = base_m / (1.0 + 0.25 * lagged * lagged + 0.5 * slope * slope)
            force = 0.5 * (shift_down(lagged) - shift_up(lagged))
            balance_m, weights = flow_terms(disp, stiff, solid)
            disp = disp + 0.8 * (force + balance_m - 0.5 * disp) / (weights + 0.5)
        if macro + 1 < MACRO:
            heat = plastic(disp)
            lagged = temp
    return jnp.stack([temp, disp])
```

```python
import functools

import jax
import jax.numpy as jnp
from jax import lax
from jax.experimental import pallas as pl
from jax.experimental.pallas import tpu as pltpu
from jax.sharding import PartitionSpec as P

MESH = pl.DeviceIdType.MESH
BRICK = 8
MACRO = 2
SUBS = 4
NSRC = 16
H = 4
BX, BY, NZ = 32, 16, 128
PR = BY + 2 * H
NP = BX + 2 * H
BASE = 32
ROWS = BASE + NP * PR + 32
DIRS = ((-1, 0), (1, 0), (0, -1), (0, 1), (-1, -1), (-1, 1), (1, -1), (1, 1))
OPP = tuple(DIRS.index((-dx, -dy)) for dx, dy in DIRS)
OWN0, BASE0, PART0, OWN1, PART1 = range(5)


def plane(xp):
    return pl.multiple_of(BASE + PR * xp, 8)


def z_next(value, last):
    return jnp.where(last, 0.0, pltpu.roll(value, NZ - 1, 1))


def z_prev(value, first):
    return jnp.where(first, 0.0, pltpu.roll(value, 1, 1))


def lane_ends(rows):
    lane = lax.broadcasted_iota(jnp.int32, (rows, NZ), 1)
    return lane == 0, lane == NZ - 1


def kernel(
    state, coef, mask, bricks, powers, out,
    fu, fb, fl, fk, fq, fa, ff, fm, src, newb, ypack, pbody, xland, yland, cland,
    body_send, body_recv, send, recv,
):
    team, gx, gy = lax.axis_index("team"), lax.axis_index("gx"), lax.axis_index("gy")
    ngx, ngy = lax.axis_size("gx"), lax.axis_size("gy")
    partner = (1 - team, gx, gy)

    def exists(d):
        dx, dy = DIRS[d]
        ok = None
        for delta, pos, size in ((dx, gx, ngx), (dy, gy, ngy)):
            if delta:
                this = pos > 0 if delta < 0 else pos < size - 1
                ok = this if ok is None else jnp.logical_and(ok, this)
        return ok

    def near(d):
        return (team, gx + DIRS[d][0], gy + DIRS[d][1])

    barrier = pltpu.get_barrier_semaphore()
    pl.semaphore_signal(barrier, inc=1, device_id=partner, device_id_type=MESH)
    count = jnp.int32(1)
    for d in range(8):
        @pl.when(exists(d))
        def _():
            pl.semaphore_signal(barrier, inc=1, device_id=near(d), device_id_type=MESH)
        count = count + exists(d).astype(jnp.int32)
    pl.semaphore_wait(barrier, count)

    def body_copy(source, m):
        return pltpu.make_async_remote_copy(
            src_ref=source, dst_ref=pbody.at[m], send_sem=body_send.at[m],
            recv_sem=body_recv.at[m], device_id=partner, device_id_type=MESH,
        )

    def strip(ref_body, kind, d):
        dx, dy = DIRS[d]
        o = OPP[d]
        if dy == 0:
            source = ref_body.at[pl.ds(0 if dx < 0 else BX - H, H)]
            target = xland.at[kind, o]
        elif dx == 0:
            source = ypack.at[kind, d - 2]
            target = yland.at[kind, o - 2]
        else:
            source = ypack.at[kind, 0 if dy < 0 else 1, pl.ds(0 if dx < 0 else (BX - H) * H, H * H)]
            target = cland.at[kind, o - 4]
        return pltpu.make_async_remote_copy(
            src_ref=source, dst_ref=target, send_sem=send.at[kind, d],
            recv_sem=recv.at[kind, o], device_id=near(d), device_id_type=MESH,
        )

    def pack(ref_body, kind):
        @pl.loop(0, BX // 8)
        def _(i):
            for j in range(8):
                x = i * 8 + j
                ypack[kind, 0, pl.ds(pl.multiple_of(i * 32, 32) + 4 * j, H), :] = ref_body[x, 0:H, :]
                ypack[kind, 1, pl.ds(pl.multiple_of(i * 32, 32) + 4 * j, H), :] = ref_body[x, BY - H:BY, :]

    def start_strips(ref_body, kind):
        for d in range(8):
            @pl.when(exists(d))
            def _():
                strip(ref_body, kind, d).start()

    def wait_strips(ref_body, kind):
        for d in range(8):
            @pl.when(exists(d))
            def _():
                recv_wait(kind, d)

    def recv_wait(kind, d):
        dx, dy = DIRS[d]
        if dy == 0:
            ref = xland.at[kind, d]
        elif dx == 0:
            ref = yland.at[kind, d - 2]
        else:
            ref = cland.at[kind, d - 4]
        pltpu.make_async_remote_copy(
            src_ref=ref, dst_ref=ref, send_sem=send.at[kind, d], recv_sem=recv.at[kind, d],
            device_id=near(d), device_id_type=MESH,
        ).wait_recv()

    def wait_sent(ref_body, kind):
        for d in range(8):
            @pl.when(exists(d))
            def _():
                strip(ref_body, kind, d).wait_send()

    def unpack_body(ref_body, flat):
        @pl.loop(0, BX // 4)
        def _(i):
            for j in range(4):
                flat[pl.ds(plane(i * 4 + j + H) + H, BY), :] = ref_body[i * 4 + j]

    def unpack_strips(kind, flat):
        for d in range(8):
            dx, dy = DIRS[d]

            @pl.when(exists(d))
            def _():
                row = 0 if dy < 0 else PR - H
                first = 0 if dx < 0 else NP - H
                if dy == 0:
                    for j in range(H):
                        flat[pl.ds(BASE + PR * (first + j) + H, BY), :] = xland[kind, d, j]
                elif dx == 0:
                    @pl.loop(0, BX // 8)
                    def _(i):
                        for j in range(8):
                            flat[pl.ds(plane(i * 8 + j + H) + row, H), :] = yland[
                                kind, d - 2, pl.ds(pl.multiple_of(i * 32, 32) + 4 * j, H), :
                            ]
                else:
                    for j in range(H):
                        flat[pl.ds(BASE + PR * (first + j) + row, H), :] = cland[
                            kind, d - 4, pl.ds(4 * j, H), :
                        ]

    own = state.at[0]
    body_copy(own, 0).start()
    pack(own, OWN0)
    start_strips(own, OWN0)

    segment = lax.broadcasted_iota(jnp.int32, (NZ // BRICK, NZ), 0)
    spread = (lax.broadcasted_iota(jnp.int32, (NZ // BRICK, NZ), 1) // BRICK == segment).astype(jnp.float32)

    @pl.loop(0, BX // 8)
    def _(i):
        flags = (mask[pl.ds(i * 8, 8)] == 1).astype(jnp.float32).reshape(8 * BY, NZ // BRICK)
        lit = jnp.dot(flags, spread, preferred_element_type=jnp.float32)
        active = jnp.where(lit > 0.5, 1.0, 0.05)
        newb[0, pl.ds(i * 8, 8)] = coef[0, pl.ds(i * 8, 8)] * active.reshape(8, BY, NZ)

    pack(newb.at[0], BASE0)
    start_strips(newb.at[0], BASE0)

    zeros = jnp.zeros((64, NZ), jnp.float32)

    @pl.loop(0, ROWS // 64)
    def _(i):
        at = pl.ds(pl.multiple_of(i * 64, 64), 64)
        fu[0, at, :] = zeros
        fu[1, at, :] = zeros
        fb[at, :] = zeros
        fl[at, :] = zeros
        fk[at, :] = zeros
        fq[at, :] = zeros
        fm[at, :] = zeros

    unpack_body(own, fu.at[0])
    unpack_body(newb.at[0], fb)

    row = lax.broadcasted_iota(jnp.int32, (PR, NZ), 0)
    low = jnp.where(gy == 0, H, 0)
    high = jnp.where(gy == ngy - 1, PR - H, PR)
    factor = jnp.where(team == 0, 0.025, 0.8)
    inside = jnp.where(jnp.logical_and(row >= low, row < high), factor, 0.0)

    @pl.loop(jnp.where(gx == 0, H, 0), jnp.where(gx == ngx - 1, NP - H, NP))
    def _(xp):
        fm[pl.ds(plane(xp), PR), :] = inside

    nbz = NZ // BRICK
    nby = ngy * (BY // BRICK)

    @pl.when(team == 0)
    def _():
        lane_brick = lax.broadcasted_iota(jnp.int32, (PR, NZ), 1) // BRICK
        row_brick = gy * (BY // BRICK) + (row + BRICK - H) // BRICK - 1
        first_x = gx * (BX // BRICK) - 1

        @pl.loop(0, MACRO * SUBS)
        def _(g):
            acc = [jnp.zeros((PR, NZ), jnp.float32) for _ in range(BX // BRICK + 2)]
            for i in range(NSRC):
                b = bricks[g, i]
                p = 2.0 * powers[g, i]
                here = jnp.where(
                    jnp.logical_and(lane_brick == b % nbz, row_brick == (b // nbz) % nby), p, 0.0
                )
                bx = b // (nbz * nby) - first_x
                acc = [a + jnp.where(bx == j, here, 0.0) for j, a in enumerate(acc)]
            for j, a in enumerate(acc):
                src[g, j] = a

    def thermal_prepare():
        _, last = lane_ends(2 * PR)

        @pl.loop(0, NP // 2)
        def _(i):
            at = pl.ds(plane(2 * i), 2 * PR)
            w = fl[at, :]
            slope = z_next(w, last) - w
            fa[at, :] = slope * slope

    def solid_prepare():
        first, last = lane_ends(2 * PR)

        @pl.loop(0, NP // 2)
        def _(i):
            at = pl.ds(plane(2 * i), 2 * PR)
            w = fl[at, :]
            fa[at, :] = 2.0 + 0.5 * w * w
            ff[at, :] = 6.0 * (z_next(w, last) - z_prev(w, first))

    def thermal_step(index, s, cur, nxt, final):
        r = H - 1 - s
        first, last = lane_ends(2 * PR)

        @pl.loop(0, (BX + 2 * r + 2) // 2)
        def _(i):
            at = pl.ds(plane(2 * i + H - r - 1), 2 * PR)
            t = fu[cur, at, :]
            k = fb[at, :] * (1.0 + 0.5 * jnp.tanh(t))
            fk[at, :] = k
            fq[at, :] = k * t

        def update(at0, rows, first, last, heating):
            def faces(load, mid):
                return (
                    (load(-PR) + load(PR)) + (load(-1) + load(1))
                    + (z_next(mid, last) + z_prev(mid, first))
                )
            lu = lambda o: fu[cur, pl.ds(at0 + o, rows), :]
            lk = lambda o: fk[pl.ds(at0 + o, rows), :]
            lq = lambda o: fq[pl.ds(at0 + o, rows), :]
            t, k, q = lu(0), lk(0), lq(0)
            flow = k * faces(lu, t) + faces(lq, q) - t * (6.0 * k + faces(lk, k))
            return t + fm[pl.ds(at0, rows), :] * (flow + heating + fa[pl.ds(at0, rows), :])

        def brick_of(xp):
            return (xp + BRICK - H) // BRICK

        if not final:
            @pl.loop(0, (BX + 2 * r) // 2)
            def _(i):
                xp = 2 * i + H - r
                heating = jnp.concatenate([src[index, brick_of(xp)], src[index, brick_of(xp + 1)]], axis=0)
                fu[nxt, pl.ds(plane(xp), 2 * PR), :] = update(plane(xp), 2 * PR, first, last, heating)
        else:
            f1, l1 = lane_ends(BY)

            @pl.loop(0, BX // 2)
            def _(i):
                for j in range(2):
                    xp = 2 * i + j + H
                    heating = src[index, brick_of(xp), H:H + BY]
                    final[xp - H] = update(plane(xp) + H, BY, f1, l1, heating)

    def solid_step(s, cur, nxt, final):
        r = H - 1 - s
        first, last = lane_ends(2 * PR)

        @pl.loop(0, (BX + 2 * r + 2) // 2)
        def _(i):
            at = pl.ds(plane(2 * i + H - r - 1), 2 * PR)
            u = fu[cur, at, :]
            slope = z_next(u, last) - u
            k = 2.0 * fb[at, :] / (fa[at, :] + slope * slope)
            fk[at, :] = k
            fq[at, :] = k * u

        def update(at0, rows, first, last):
            def solid(load):
                p = load(-PR) + load(PR)
                q = load(-1) + load(1)
                e = (load(-PR - 1) + load(-PR + 1)) + (load(PR - 1) + load(PR + 1))
                h = p + q + 0.5 * e
                return e + z_next(h, last) + z_prev(h, first)
            lu = lambda o: fu[cur, pl.ds(at0 + o, rows), :]
            lk = lambda o: fk[pl.ds(at0 + o, rows), :]
            lq = lambda o: fq[pl.ds(at0 + o, rows), :]
            u, k = lu(0), lk(0)
            top = ff[pl.ds(at0, rows), :] + k * solid(lu) + solid(lq)
            bottom = 16.0 * k + solid(lk) + 6.0
            return 0.2 * u + fm[pl.ds(at0, rows), :] * (top / bottom)

        if not final:
            @pl.loop(0, (BX + 2 * r) // 2)
            def _(i):
                xp = 2 * i + H - r
                fu[nxt, pl.ds(plane(xp), 2 * PR), :] = update(plane(xp), 2 * PR, first, last)
        else:
            f1, l1 = lane_ends(BY)

            @pl.loop(0, BX // 2)
            def _(i):
                for j in range(2):
                    xp = 2 * i + j + H
                    final[xp - H] = update(plane(xp) + H, BY, f1, l1)

    def macro_step(m, final):
        @pl.when(team == 0)
        def _():
            thermal_prepare()
            for s in range(SUBS):
                thermal_step(m * SUBS + s, s, s % 2, 1 - s % 2, final if s == SUBS - 1 else None)

        @pl.when(team == 1)
        def _():
            solid_prepare()
            for s in range(SUBS):
                solid_step(s, s % 2, 1 - s % 2, final if s == SUBS - 1 else None)

    def forward(m, kind):
        body_copy(pbody.at[m], m).wait_recv()
        pack(pbody.at[m], kind)
        start_strips(pbody.at[m], kind)
        unpack_body(pbody.at[m], fl)

    forward(0, PART0)
    wait_strips(own, OWN0)
    unpack_strips(OWN0, fu.at[0])
    wait_strips(newb.at[0], BASE0)
    unpack_strips(BASE0, fb)
    wait_strips(own, PART0)
    unpack_strips(PART0, fl)
    mid = newb.at[1]
    macro_step(0, mid)

    body_copy(mid, 1).start()
    pack(mid, OWN1)
    start_strips(mid, OWN1)
    unpack_body(mid, fu.at[0])
    wait_strips(mid, OWN1)
    unpack_strips(OWN1, fu.at[0])
    forward(1, PART1)
    wait_strips(mid, PART1)
    unpack_strips(PART1, fl)
    macro_step(1, out.at[0])

    body_copy(own, 0).wait_send()
    body_copy(mid, 1).wait_send()
    wait_sent(own, OWN0)
    wait_sent(newb.at[0], BASE0)
    wait_sent(pbody.at[0], PART0)
    wait_sent(mid, OWN1)
    wait_sent(pbody.at[1], PART1)


def local(state, coef, mask, src_brick, power):
    vmem = pl.BlockSpec(memory_space=pltpu.VMEM)
    smem = pl.BlockSpec(memory_space=pltpu.SMEM)
    flat = pltpu.VMEM((ROWS, NZ), jnp.float32)
    return pl.pallas_call(
        kernel,
        name="fields",
        out_shape=jax.ShapeDtypeStruct((1, BX, BY, NZ), jnp.float32),
        in_specs=[vmem, vmem, vmem, smem, smem],
        out_specs=vmem,
        scratch_shapes=[
            pltpu.VMEM((2, ROWS, NZ), jnp.float32),
            flat, flat, flat, flat, flat, flat, flat,
            pltpu.VMEM((MACRO * SUBS, BX // BRICK + 2, PR, NZ), jnp.float32),
            pltpu.VMEM((2, BX, BY, NZ), jnp.float32),
            pltpu.VMEM((5, 2, BX * H, NZ), jnp.float32),
            pltpu.VMEM((2, BX, BY, NZ), jnp.float32),
            pltpu.VMEM((5, 2, H, BY, NZ), jnp.float32),
            pltpu.VMEM((5, 2, BX * H, NZ), jnp.float32),
            pltpu.VMEM((5, 4, H * H, NZ), jnp.float32),
            pltpu.SemaphoreType.DMA((2,)),
            pltpu.SemaphoreType.DMA((2,)),
            pltpu.SemaphoreType.DMA((5, 8)),
            pltpu.SemaphoreType.DMA((5, 8)),
        ],
        compiler_params=pltpu.CompilerParams(
            collective_id=0, has_side_effects=True, vmem_limit_bytes=40 * 2**20
        ),
    )(state, coef, mask, src_brick, power)


def solution(mesh):
    placed = (P("team", "gx", "gy", None), P("team", "gx", "gy", None), P("gx", "gy", None), P(), P())
    return jax.shard_map(
        local, mesh=mesh, in_specs=placed, out_specs=P("team", "gx", "gy", None), check_vma=False
    )
```

```python
import jax
import jax.numpy as jnp
from jax import lax
from jax.experimental import pallas as pl
from jax.experimental.pallas import tpu as pltpu
from jax.sharding import PartitionSpec as P

MESH = pl.DeviceIdType.MESH
BRICK = 8
MACRO = 2
SUBS = 4
NSRC = 16
H = 4
BX, BY, NZ = 32, 16, 128
PR = BY + 2 * H
NP = BX + 2 * H
BASE = 32
ROWS = BASE + NP * PR + 32
CHUNK = 192
DIRS = ((-1, 0), (1, 0), (0, -1), (0, 1), (-1, -1), (-1, 1), (1, -1), (1, 1))
OPP = tuple(DIRS.index((-dx, -dy)) for dx, dy in DIRS)
OWN0, BASE0, PART0, OWN1, PART1 = range(5)

PIECES = ((0, H), (BX - H, H), (H, BX - 2 * H))


def row_of(xp):
    return BASE + PR * xp


def z_next(value):
    lane = lax.broadcasted_iota(jnp.int32, value.shape, 1)
    return jnp.where(lane == NZ - 1, 0.0, pltpu.roll(value, NZ - 1, 1))


def z_prev(value):
    lane = lax.broadcasted_iota(jnp.int32, value.shape, 1)
    return jnp.where(lane == 0, 0.0, pltpu.roll(value, 1, 1))


def shift_matrix():
    source = lax.broadcasted_iota(jnp.int32, (NZ, 2 * NZ), 0)
    target = lax.broadcasted_iota(jnp.int32, (NZ, 2 * NZ), 1)
    following = jnp.logical_and(target < NZ, source == target + 1)
    previous = jnp.logical_and(target >= NZ, source == target - NZ - 1)
    once = jnp.logical_or(following, previous).astype(jnp.bfloat16)
    return jnp.concatenate([once, once], axis=0)


def z_both(value, matrix):
    high = value.astype(jnp.bfloat16)
    rest = (value - high.astype(jnp.float32)).astype(jnp.bfloat16)
    both = jnp.dot(jnp.concatenate([high, rest], axis=1), matrix, preferred_element_type=jnp.float32)
    return both[:, :NZ], both[:, NZ:]


def kernel(
    state, coef, mask_in, bricks_in, powers_in, out,
    fu, fb, fl, vz, fa, ff, fm, src, sv, cv, nb, act, pk, pb, xland, yland, cland, mask, bricks, powers,
    local_sem, body_send, body_recv, send, recv,
):
    team, gx, gy = lax.axis_index("team"), lax.axis_index("gx"), lax.axis_index("gy")
    ngx, ngy = lax.axis_size("gx"), lax.axis_size("gy")
    partner = (1 - team, gx, gy)

    state_copy = pltpu.make_async_copy(state.at[0], sv, local_sem.at[0])
    coef_copy = pltpu.make_async_copy(coef.at[0], cv, local_sem.at[1])
    mask_copy = pltpu.make_async_copy(mask_in, mask, local_sem.at[2])
    brick_copy = pltpu.make_async_copy(bricks_in, bricks, local_sem.at[3])
    power_copy = pltpu.make_async_copy(powers_in, powers, local_sem.at[4])
    state_copy.start()
    coef_copy.start()
    mask_copy.start()
    brick_copy.start()
    power_copy.start()

    def exists(d):
        dx, dy = DIRS[d]
        ok = None
        for delta, pos, size in ((dx, gx, ngx), (dy, gy, ngy)):
            if delta:
                this = pos > 0 if delta < 0 else pos < size - 1
                ok = this if ok is None else jnp.logical_and(ok, this)
        return ok

    def near(d, crossed=False):
        return (1 - team if crossed else team, gx + DIRS[d][0], gy + DIRS[d][1])

    barrier = pltpu.get_barrier_semaphore()
    pl.semaphore_signal(barrier, inc=1, device_id=partner, device_id_type=MESH)
    count = jnp.int32(1)
    for d in range(8):
        @pl.when(exists(d))
        def _():
            pl.semaphore_signal(barrier, inc=1, device_id=near(d), device_id_type=MESH)
            if d >= 2:
                pl.semaphore_signal(barrier, inc=1, device_id=near(d, True), device_id_type=MESH)
        count = count + (2 if d >= 2 else 1) * exists(d).astype(jnp.int32)

    def body_copy(source, m, piece):
        first, planes = PIECES[piece]
        return pltpu.make_async_remote_copy(
            src_ref=source.at[pl.ds(first, planes)], dst_ref=pb.at[m, pl.ds(first, planes)],
            send_sem=body_send.at[m, piece], recv_sem=body_recv.at[m, piece],
            device_id=partner, device_id_type=MESH,
        )

    strips = {
        OWN0: (sv, pk.at[0], False),
        BASE0: (cv, pk.at[2], False),
        PART0: (pb.at[0], pk.at[0], True),
        OWN1: (nb, pk.at[1], False),
        PART1: (pb.at[1], pk.at[1], True),
    }
    ALONG_Y = (2, 3, 4, 5, 6, 7)

    def strip(kind, d):
        block, packed, crossed = strips[kind]
        dx, dy = DIRS[d]
        o = OPP[d]
        if dy == 0:
            source = block.at[pl.ds(0 if dx < 0 else BX - H, H)]
            target = xland.at[kind, o]
        elif dx == 0:
            source = packed.at[d - 2]
            target = yland.at[kind, o - 2]
        else:
            source = packed.at[0 if dy < 0 else 1, pl.ds(0 if dx < 0 else (BX - H) * H, H * H)]
            target = cland.at[kind, o - 4]
        return pltpu.make_async_remote_copy(
            src_ref=source, dst_ref=target, send_sem=send.at[kind, d],
            recv_sem=recv.at[kind, o], device_id=near(d, crossed and d >= 2), device_id_type=MESH,
        )

    def start_strips(kind, ways):
        for d in ways:
            @pl.when(exists(d))
            def _():
                strip(kind, d).start()

    def landing(kind, d):
        return xland.at[kind, d] if d < 2 else yland.at[kind, d - 2] if d < 4 else cland.at[kind, d - 4]

    def receive_strips(kind, flat):
        for d in (0, 1) + ALONG_Y:
            dx, dy = DIRS[d]

            @pl.when(exists(d))
            def _():
                ref = landing(kind, d)
                pltpu.make_async_remote_copy(
                    src_ref=ref, dst_ref=ref, send_sem=send.at[kind, d], recv_sem=recv.at[kind, d],
                    device_id=near(d), device_id_type=MESH,
                ).wait_recv()
                row = 0 if dy < 0 else PR - H
                first = 0 if dx < 0 else NP - H
                if dy == 0:
                    for j in range(H):
                        flat[pl.ds(row_of(first + j) + H, BY), :] = xland[kind, d, j]
                elif dx == 0:
                    for x in range(BX):
                        flat[pl.ds(row_of(x + H) + row, H), :] = yland[kind, d - 2, pl.ds(H * x, H), :]
                else:
                    for j in range(H):
                        flat[pl.ds(row_of(first + j) + row, H), :] = cland[kind, d - 4, pl.ds(H * j, H), :]

    def wait_sent(kind):
        for d in range(8):
            @pl.when(exists(d))
            def _():
                strip(kind, d).wait_send()

    def pack(slot, block):
        for x in range(BX):
            pk[slot, 0, pl.ds(H * x, H), :] = block[x, 0:H, :]
            pk[slot, 1, pl.ds(H * x, H), :] = block[x, BY - H:BY, :]

    def send_block(block, slot, m, own, other):
        body_copy(block, m, 0).start()
        body_copy(block, m, 1).start()
        pack(slot, block)
        start_strips(other, ALONG_Y)
        start_strips(own, ALONG_Y + (0, 1))
        body_copy(block, m, 2).start()

    def forward(m, kind):
        for side in range(2):
            body_copy(nb, m, side).wait_recv()
            start_strips(kind, (side,))

    def unpack_partner(m):
        body_copy(nb, m, 2).wait_recv()
        for x in range(BX):
            fl[pl.ds(row_of(x + H) + H, BY), :] = pb[m, x]

    state_copy.wait()
    pl.semaphore_wait(barrier, count)
    send_block(sv, 0, 0, OWN0, PART0)

    segment = lax.broadcasted_iota(jnp.int32, (NZ // BRICK, NZ), 0)
    spread = (lax.broadcasted_iota(jnp.int32, (NZ // BRICK, NZ), 1) // BRICK == segment).astype(jnp.float32)
    unit = jnp.where(team == 0, 1.0, 2.0)
    mask_copy.wait()
    for y in range(BY):
        lit = lax.dot_general(
            (mask[y] == 1).astype(jnp.float32), spread, (((0,), (0,)), ((), ())),
            preferred_element_type=jnp.float32,
        )
        act[pl.ds(y * BX, BX), :] = jnp.where(lit > 0.5, unit, 0.05 * unit)
    coef_copy.wait()
    for x in range(BX):
        cv[x] = cv[x] * act[pl.ds(x, BY, stride=BX), :]
    pack(2, cv)
    start_strips(BASE0, ALONG_Y + (0, 1))

    zeros = jnp.zeros((64, NZ), jnp.float32)

    @pl.loop(0, ROWS // 64)
    def _(i):
        at = pl.ds(pl.multiple_of(i * 64, 64), 64)
        fu[0, at, :] = zeros
        fu[1, at, :] = zeros
        fb[at, :] = zeros
        fl[at, :] = zeros
        fm[at, :] = zeros

    for x in range(BX):
        at = pl.ds(row_of(x + H) + H, BY)
        fu[0, at, :] = sv[x]
        fb[at, :] = cv[x]

    row = lax.broadcasted_iota(jnp.int32, (PR, NZ), 0)
    low = jnp.where(gy == 0, H, 0)
    high = jnp.where(gy == ngy - 1, PR - H, PR)
    factor = jnp.where(team == 0, 0.025, 0.8)
    inside = jnp.where(jnp.logical_and(row >= low, row < high), factor, 0.0)

    @pl.loop(jnp.where(gx == 0, H, 0), jnp.where(gx == ngx - 1, NP - H, NP))
    def _(xp):
        fm[pl.ds(pl.multiple_of(row_of(xp), 8), PR), :] = inside

    forward(0, PART0)
    brick_copy.wait()
    power_copy.wait()

    nbz = NZ // BRICK
    nby = ngy * (BY // BRICK)

    @pl.when(team == 0)
    def _():
        lane_brick = lax.broadcasted_iota(jnp.int32, (PR, NZ), 1) // BRICK
        row_brick = gy * (BY // BRICK) + (row + BRICK - H) // BRICK - 1
        first_x = gx * (BX // BRICK) - 1

        @pl.loop(0, MACRO * SUBS)
        def _(g):
            acc = [jnp.zeros((PR, NZ), jnp.float32) for _ in range(BX // BRICK + 2)]
            for i in range(NSRC):
                b = bricks[g, i]
                p = 2.0 * powers[g, i]
                here = jnp.where(
                    jnp.logical_and(lane_brick == b % nbz, row_brick == (b // nbz) % nby), p, 0.0
                )
                bx = b // (nbz * nby) - first_x
                acc = [a + jnp.where(bx == j, here, 0.0) for j, a in enumerate(acc)]
            for j, a in enumerate(acc):
                src[g, j] = a

    unpack_partner(0)
    receive_strips(OWN0, fu.at[0])
    receive_strips(BASE0, fb)
    receive_strips(PART0, fl)

    matrix = shift_matrix()

    def thermal_prepare():
        for i in range(NP * PR // CHUNK):
            at = pl.ds(BASE + CHUNK * i, CHUNK)
            w = fl[at, :]
            slope = z_next(w) - w
            fa[at, :] = slope * slope

    def solid_prepare():
        for i in range(NP * PR // CHUNK):
            at = pl.ds(BASE + CHUNK * i, CHUNK)
            w = fl[at, :]
            fa[at, :] = 2.0 + 0.5 * w * w
            ff[at, :] = 6.0 * (z_next(w) - z_prev(w))

    def lateral(parts, finish):
        for c in range(PR // 8):
            window = [parts(x, c) for x in (0, 1)]
            for x in range(1, NP - 1):
                window.append(parts(x + 1, c))
                below, here, above = window
                finish(x, c, [lo[0] + hi[0] + me[1] for lo, me, hi in zip(below, here, above)])
                window.pop(0)

    def thermal_step(g, cur, nxt):
        for i in range(NP * PR // CHUNK):
            at = pl.ds(BASE + CHUNK * i, CHUNK)
            t = fu[cur, at, :]
            tp, tn = z_next(t), z_prev(t)
            k = fb[at, :] * (1.0 + 0.5 * jnp.tanh(t))
            kp, kn = z_both(k, matrix)
            vz[0, at, :] = k
            vz[1, at, :] = k * t
            vz[2, at, :] = tp + tn
            vz[3, at, :] = kp + kn
            vz[4, at, :] = kp * tp + kn * tn

        def parts(x, c):
            at = row_of(x) + 8 * c
            found = []
            for load, z in ((lambda r: fu[cur, pl.ds(r, 8), :], 2), (lambda r: vz[0, pl.ds(r, 8), :], 3),
                            (lambda r: vz[1, pl.ds(r, 8), :], 4)):
                found.append((load(at), load(at - 1) + load(at + 1) + vz[z, pl.ds(at, 8), :]))
            return found

        def finish(x, c, sums):
            at = pl.ds(row_of(x) + 8 * c, 8)
            t, k = fu[cur, at, :], vz[0, at, :]
            flow = k * sums[0] + sums[2] - t * (6.0 * k + sums[1])
            heating = src[g, (x + BRICK - H) // BRICK, pl.ds(8 * c, 8), :]
            fu[nxt, at, :] = t + fm[at, :] * (flow + heating + fa[at, :])

        lateral(parts, finish)

    def solid_step(cur, nxt):
        for i in range(NP * PR // CHUNK):
            at = pl.ds(BASE + CHUNK * i, CHUNK)
            u = fu[cur, at, :]
            up, un = z_next(u), z_prev(u)
            slope = up - u
            k = fb[at, :] / (fa[at, :] + slope * slope)
            kp, kn = z_both(k, matrix)
            for j, (value, both) in enumerate(((u, up + un), (k, kp + kn), (k * u, kp * up + kn * un))):
                vz[2 * j, at, :] = value + 0.5 * both
                vz[2 * j + 1, at, :] = both
            vz[6, at, :] = k

        def parts(x, c):
            at = row_of(x) + 8 * c
            found = []
            for j in range(3):
                whole = lambda r: vz[2 * j, pl.ds(r, 8), :]
                both = lambda r: vz[2 * j + 1, pl.ds(r, 8), :]
                found.append((whole(at - 1) + whole(at + 1) + both(at), both(at - 1) + both(at + 1)))
            return found

        def finish(x, c, sums):
            at = pl.ds(row_of(x) + 8 * c, 8)
            u, k = fu[cur, at, :], vz[6, at, :]
            top = ff[at, :] + k * sums[0] + sums[2]
            bottom = 16.0 * k + sums[1] + 6.0
            fu[nxt, at, :] = 0.2 * u + fm[at, :] * (top / bottom)

        lateral(parts, finish)

    @pl.loop(0, MACRO)
    def _(m):
        @pl.when(team == 0)
        def _():
            thermal_prepare()

            @pl.loop(0, SUBS // 2)
            def _(i):
                thermal_step(m * SUBS + 2 * i, 0, 1)
                thermal_step(m * SUBS + 2 * i + 1, 1, 0)

        @pl.when(team == 1)
        def _():
            solid_prepare()

            @pl.loop(0, SUBS // 2)
            def _(i):
                solid_step(0, 1)
                solid_step(1, 0)

        @pl.when(m == 0)
        def _():
            for x in range(BX):
                nb[x] = fu[0, pl.ds(row_of(x + H) + H, BY), :]
            send_block(nb, 1, 1, OWN1, PART1)
            forward(1, PART1)
            unpack_partner(1)
            receive_strips(OWN1, fu.at[0])
            receive_strips(PART1, fl)

    for x in range(BX):
        out[0, x] = fu[0, pl.ds(row_of(x + H) + H, BY), :]

    for m in range(MACRO):
        for piece in range(3):
            body_copy(nb, m, piece).wait_send()
    for kind in range(5):
        wait_sent(kind)


def local(state, coef, mask, src_brick, power):
    vmem = pl.BlockSpec(memory_space=pltpu.VMEM)
    hbm = pl.BlockSpec(memory_space=pltpu.HBM)
    flat = pltpu.VMEM((ROWS, NZ), jnp.float32)
    block = pltpu.VMEM((BX, BY, NZ), jnp.float32)
    return pl.pallas_call(
        kernel,
        name="fields",
        out_shape=jax.ShapeDtypeStruct((1, BX, BY, NZ), jnp.float32),
        in_specs=[hbm] * 5,
        out_specs=vmem,
        scratch_shapes=[
            pltpu.VMEM((2, ROWS, NZ), jnp.float32),
            flat, flat,
            pltpu.VMEM((7, ROWS, NZ), jnp.float32),
            flat, flat, flat,
            pltpu.VMEM((MACRO * SUBS, BX // BRICK + 2, PR, NZ), jnp.float32),
            block, block, block,
            pltpu.VMEM((BY * BX, NZ), jnp.float32),
            pltpu.VMEM((3, 2, BX * H, NZ), jnp.float32),
            pltpu.VMEM((2, BX, BY, NZ), jnp.float32),
            pltpu.VMEM((5, 2, H, BY, NZ), jnp.float32),
            pltpu.VMEM((5, 2, BX * H, NZ), jnp.float32),
            pltpu.VMEM((5, 4, H * H, NZ), jnp.float32),
            pltpu.VMEM((BY, NZ // BRICK, BX), jnp.int32),
            pltpu.SMEM((MACRO * SUBS, NSRC), jnp.int32),
            pltpu.SMEM((MACRO * SUBS, NSRC), jnp.float32),
            pltpu.SemaphoreType.DMA((5,)),
            pltpu.SemaphoreType.DMA((2, 3)),
            pltpu.SemaphoreType.DMA((2, 3)),
            pltpu.SemaphoreType.DMA((5, 8)),
            pltpu.SemaphoreType.DMA((5, 8)),
        ],
        compiler_params=pltpu.CompilerParams(
            collective_id=0, has_side_effects=True, vmem_limit_bytes=60 * 2**20
        ),
    )(state, coef, jnp.transpose(mask, (1, 2, 0)), src_brick, power)


def solution(mesh):
    placed = (P("team", "gx", "gy", None), P("team", "gx", "gy", None), P("gx", "gy", None), P(), P())
    return jax.shard_map(
        local, mesh=mesh, in_specs=placed, out_specs=P("team", "gx", "gy", None), check_vma=False
    )
```

```python
import jax
import jax.numpy as jnp
from jax import lax
from jax.experimental import pallas as pl
from jax.experimental.pallas import tpu as pltpu
from jax.sharding import PartitionSpec as P

MESH = pl.DeviceIdType.MESH
BRICK = 8
MACRO = 2
SUBS = 4
NSRC = 16
H = 4
BX, BY, NZ = 32, 16, 128
PR = BY + 2 * H
NP = BX + 2 * H
BASE = 32
ROWS = BASE + NP * PR + 32
CHUNK = 192
DIRS = ((-1, 0), (1, 0), (0, -1), (0, 1), (-1, -1), (-1, 1), (1, -1), (1, 1))
KINDS = 5
OPP = tuple(DIRS.index((-dx, -dy)) for dx, dy in DIRS)
OWN0, BASE0, PART0, OWN1, PART1 = range(KINDS)

PIECES = ((0, H), (BX - H, H), (H, BX - 2 * H))


def row_of(xp):
    return BASE + PR * xp


def z_next(value):
    lane = lax.broadcasted_iota(jnp.int32, value.shape, 1)
    return jnp.where(lane == NZ - 1, 0.0, pltpu.roll(value, NZ - 1, 1))


def z_prev(value):
    lane = lax.broadcasted_iota(jnp.int32, value.shape, 1)
    return jnp.where(lane == 0, 0.0, pltpu.roll(value, 1, 1))


def shift_matrix():
    source = lax.broadcasted_iota(jnp.int32, (NZ, 2 * NZ), 0)
    target = lax.broadcasted_iota(jnp.int32, (NZ, 2 * NZ), 1)
    following = jnp.logical_and(target < NZ, source == target + 1)
    previous = jnp.logical_and(target >= NZ, source == target - NZ - 1)
    once = jnp.logical_or(following, previous).astype(jnp.bfloat16)
    return jnp.concatenate([once, once], axis=0)


def z_both(value, matrix):
    high = value.astype(jnp.bfloat16)
    rest = (value - high.astype(jnp.float32)).astype(jnp.bfloat16)
    both = jnp.dot(jnp.concatenate([high, rest], axis=1), matrix, preferred_element_type=jnp.float32)
    return both[:, :NZ], both[:, NZ:]


def kernel(
    state, coef, mask_in, bricks_in, powers_in, out,
    fu, fb, fl, vz, fa, ff, fm, src, sv, cv, nb, act, pk, pb, xland, yland, cland, mask, bricks, powers,
    local_sem, body_send, body_recv, send, recv,
):
    team, gx, gy = lax.axis_index("team"), lax.axis_index("gx"), lax.axis_index("gy")
    ngx, ngy = lax.axis_size("gx"), lax.axis_size("gy")
    partner = (1 - team, gx, gy)

    state_copy = pltpu.make_async_copy(state.at[0], sv, local_sem.at[0])
    coef_copy = pltpu.make_async_copy(coef.at[0], cv, local_sem.at[1])
    mask_copy = pltpu.make_async_copy(mask_in, mask, local_sem.at[2])
    brick_copy = pltpu.make_async_copy(bricks_in, bricks, local_sem.at[3])
    power_copy = pltpu.make_async_copy(powers_in, powers, local_sem.at[4])
    state_copy.start()
    coef_copy.start()
    mask_copy.start()
    brick_copy.start()
    power_copy.start()

    def exists(d):
        dx, dy = DIRS[d]
        ok = None
        for delta, pos, size in ((dx, gx, ngx), (dy, gy, ngy)):
            if delta:
                this = pos > 0 if delta < 0 else pos < size - 1
                ok = this if ok is None else jnp.logical_and(ok, this)
        return ok

    def near(d, crossed=False):
        return (1 - team if crossed else team, gx + DIRS[d][0], gy + DIRS[d][1])

    barrier = pltpu.get_barrier_semaphore()
    pl.semaphore_signal(barrier, inc=1, device_id=partner, device_id_type=MESH)
    count = jnp.int32(1)
    for d in range(4):
        @pl.when(exists(d))
        def _():
            pl.semaphore_signal(barrier, inc=1, device_id=near(d), device_id_type=MESH)
            if d >= 2:
                pl.semaphore_signal(barrier, inc=1, device_id=near(d, True), device_id_type=MESH)
        count = count + (2 if d >= 2 else 1) * exists(d).astype(jnp.int32)

    def body_copy(source, m, piece):
        first, planes = PIECES[piece]
        return pltpu.make_async_remote_copy(
            src_ref=source.at[pl.ds(first, planes)], dst_ref=pb.at[m, pl.ds(first, planes)],
            send_sem=body_send.at[m, piece], recv_sem=body_recv.at[m, piece],
            device_id=partner, device_id_type=MESH,
        )

    strips = {
        OWN0: (sv, pk.at[0], False),
        BASE0: (cv, pk.at[2], False),
        PART0: (pb.at[0], pk.at[0], True),
        OWN1: (nb, pk.at[1], False),
        PART1: (pb.at[1], pk.at[1], True),
    }
    ALONG_X, ALONG_Y = (0, 1), (2, 3)

    def strip(kind, d):
        block, packed, crossed = strips[kind]
        dx, dy = DIRS[d]
        if dy == 0:
            o = OPP[d]
            source = block.at[pl.ds(0 if dx < 0 else BX - H, H)]
            target = xland.at[kind, o]
        elif dx == 0:
            o = OPP[d]
            source = packed.at[d - 2]
            target = yland.at[kind, o - 2]
        else:
            o = DIRS.index((-dx, dy))
            source = yland.at[kind, 0 if dy < 0 else 1, pl.ds(0 if dx < 0 else (BX - H) * H, H * H)]
            target = cland.at[kind, o - 4]
        to = near(d, crossed) if dx == 0 else (team, gx + dx, gy)
        return pltpu.make_async_remote_copy(
            src_ref=source, dst_ref=target, send_sem=send.at[kind, d],
            recv_sem=recv.at[kind, o], device_id=to, device_id_type=MESH,
        )

    def start_strips(kind, ways):
        for d in ways:
            @pl.when(exists(d))
            def _():
                strip(kind, d).start()

    def landing(kind, d):
        return xland.at[kind, d] if d < 2 else yland.at[kind, d - 2] if d < 4 else cland.at[kind, d - 4]

    def arrived(kind, d):
        ref = landing(kind, d)
        pltpu.make_async_remote_copy(
            src_ref=ref, dst_ref=ref, send_sem=send.at[kind, d], recv_sem=recv.at[kind, d],
            device_id=near(d % 4), device_id_type=MESH,
        ).wait_recv()

    def relay(kind):
        for d in ALONG_Y:
            @pl.when(exists(d))
            def _():
                arrived(kind, d)
                for corner in range(4, 8):
                    if DIRS[corner][1] == DIRS[d][1]:
                        @pl.when(exists(corner))
                        def _():
                            strip(kind, corner).start()

    def receive_strips(kind, flat):
        for d in ALONG_Y + ALONG_X + (4, 5, 6, 7):
            dx, dy = DIRS[d]

            @pl.when(exists(d))
            def _():
                if d not in ALONG_Y:
                    arrived(kind, d)
                row = 0 if dy < 0 else PR - H
                first = 0 if dx < 0 else NP - H
                if dy == 0:
                    for j in range(H):
                        flat[pl.ds(row_of(first + j) + H, BY), :] = xland[kind, d, j]
                elif dx == 0:
                    for x in range(BX):
                        flat[pl.ds(row_of(x + H) + row, H), :] = yland[kind, d - 2, pl.ds(H * x, H), :]
                else:
                    for j in range(H):
                        flat[pl.ds(row_of(first + j) + row, H), :] = cland[kind, d - 4, pl.ds(H * j, H), :]

    def wait_sent(kind):
        for d in range(8):
            @pl.when(exists(d))
            def _():
                strip(kind, d).wait_send()

    def pack(slot, block):
        for x in range(BX):
            pk[slot, 0, pl.ds(H * x, H), :] = block[x, 0:H, :]
            pk[slot, 1, pl.ds(H * x, H), :] = block[x, BY - H:BY, :]

    def send_block(block, slot, m, own, other):
        body_copy(block, m, 0).start()
        body_copy(block, m, 1).start()
        pack(slot, block)
        start_strips(other, ALONG_Y)
        start_strips(own, ALONG_Y + ALONG_X)
        body_copy(block, m, 2).start()

    def forward(m, kind):
        for side in range(2):
            body_copy(nb, m, side).wait_recv()
            start_strips(kind, (side,))

    def unpack_partner(m):
        body_copy(nb, m, 2).wait_recv()
        for x in range(BX):
            fl[pl.ds(row_of(x + H) + H, BY), :] = pb[m, x]

    state_copy.wait()
    pl.semaphore_wait(barrier, count)
    send_block(sv, 0, 0, OWN0, PART0)

    segment = lax.broadcasted_iota(jnp.int32, (NZ // BRICK, NZ), 0)
    spread = (lax.broadcasted_iota(jnp.int32, (NZ // BRICK, NZ), 1) // BRICK == segment).astype(jnp.float32)
    unit = jnp.where(team == 0, 1.0, 2.0)
    mask_copy.wait()
    for y in range(BY):
        lit = lax.dot_general(
            (mask[y] == 1).astype(jnp.float32), spread, (((0,), (0,)), ((), ())),
            preferred_element_type=jnp.float32,
        )
        act[pl.ds(y * BX, BX), :] = jnp.where(lit > 0.5, unit, 0.05 * unit)
    coef_copy.wait()
    for x in range(BX):
        cv[x] = cv[x] * act[pl.ds(x, BY, stride=BX), :]
    pack(2, cv)
    start_strips(BASE0, ALONG_Y + ALONG_X)

    zeros = jnp.zeros((64, NZ), jnp.float32)

    @pl.loop(0, ROWS // 64)
    def _(i):
        at = pl.ds(pl.multiple_of(i * 64, 64), 64)
        fu[0, at, :] = zeros
        fu[1, at, :] = zeros
        fb[at, :] = zeros
        fl[at, :] = zeros
        fm[at, :] = zeros

    guard = jnp.zeros((8, NZ), jnp.float32)
    for j in range(7):
        vz[j, pl.ds(BASE - 8, 8), :] = guard
        vz[j, pl.ds(row_of(NP), 8), :] = guard

    for x in range(BX):
        at = pl.ds(row_of(x + H) + H, BY)
        fu[0, at, :] = sv[x]
        fb[at, :] = cv[x]

    row = lax.broadcasted_iota(jnp.int32, (PR, NZ), 0)
    low = jnp.where(gy == 0, H, 0)
    high = jnp.where(gy == ngy - 1, PR - H, PR)
    factor = jnp.where(team == 0, 0.025, 0.8)
    inside = jnp.where(jnp.logical_and(row >= low, row < high), factor, 0.0)

    @pl.loop(jnp.where(gx == 0, H, 0), jnp.where(gx == ngx - 1, NP - H, NP))
    def _(xp):
        fm[pl.ds(pl.multiple_of(row_of(xp), 8), PR), :] = inside

    forward(0, PART0)
    brick_copy.wait()
    power_copy.wait()

    nbz = NZ // BRICK
    nby = ngy * (BY // BRICK)

    @pl.when(team == 0)
    def _():
        lane_brick = lax.broadcasted_iota(jnp.int32, (PR, NZ), 1) // BRICK
        row_brick = gy * (BY // BRICK) + (row + BRICK - H) // BRICK - 1
        first_x = gx * (BX // BRICK) - 1

        @pl.loop(0, MACRO * SUBS)
        def _(g):
            acc = [jnp.zeros((PR, NZ), jnp.float32) for _ in range(BX // BRICK + 2)]
            for i in range(NSRC):
                b = bricks[g, i]
                p = 2.0 * powers[g, i]
                here = jnp.where(
                    jnp.logical_and(lane_brick == b % nbz, row_brick == (b // nbz) % nby), p, 0.0
                )
                bx = b // (nbz * nby) - first_x
                acc = [a + jnp.where(bx == j, here, 0.0) for j, a in enumerate(acc)]
            for j, a in enumerate(acc):
                src[g, j] = a

    relay(OWN0)
    relay(PART0)
    relay(BASE0)
    receive_strips(OWN0, fu.at[0])
    receive_strips(BASE0, fb)
    unpack_partner(0)
    receive_strips(PART0, fl)

    matrix = shift_matrix()

    def thermal_prepare():
        for i in range(NP * PR // CHUNK):
            at = pl.ds(BASE + CHUNK * i, CHUNK)
            w = fl[at, :]
            slope = z_next(w) - w
            fa[at, :] = slope * slope

    def solid_prepare():
        for i in range(NP * PR // CHUNK):
            at = pl.ds(BASE + CHUNK * i, CHUNK)
            w = fl[at, :]
            fa[at, :] = 2.0 + 0.5 * w * w
            ff[at, :] = 6.0 * (z_next(w) - z_prev(w))

    def lateral(parts, finish):
        @pl.loop(0, PR // 8)
        def _(c):
            window = [parts(x, c) for x in (0, 1)]
            for x in range(1, NP - 1):
                window.append(parts(x + 1, c))
                below, here, above = window
                finish(x, c, [lo[0] + hi[0] + me[1] for lo, me, hi in zip(below, here, above)])
                window.pop(0)

    def thermal_step(g, cur, nxt):
        for i in range(NP * PR // CHUNK):
            at = pl.ds(BASE + CHUNK * i, CHUNK)
            t = fu[cur, at, :]
            tp, tn = z_next(t), z_prev(t)
            k = fb[at, :] * (1.0 + 0.5 * jnp.tanh(t))
            kp, kn = z_both(k, matrix)
            vz[0, at, :] = k
            vz[1, at, :] = k * t
            vz[2, at, :] = tp + tn
            vz[3, at, :] = kp + kn
            vz[4, at, :] = kp * tp + kn * tn

        def parts(x, c):
            at = pl.multiple_of(row_of(x) + 8 * c, 8)
            found = []
            for load, z in ((lambda r: fu[cur, pl.ds(r, 8), :], 2), (lambda r: vz[0, pl.ds(r, 8), :], 3),
                            (lambda r: vz[1, pl.ds(r, 8), :], 4)):
                found.append((load(at), load(at - 1) + load(at + 1) + vz[z, pl.ds(at, 8), :]))
            return found

        def finish(x, c, sums):
            at = pl.ds(pl.multiple_of(row_of(x) + 8 * c, 8), 8)
            t, k = fu[cur, at, :], vz[0, at, :]
            flow = k * sums[0] + sums[2] - t * (6.0 * k + sums[1])
            heating = src[g, (x + BRICK - H) // BRICK, pl.ds(pl.multiple_of(8 * c, 8), 8), :]
            fu[nxt, at, :] = t + fm[at, :] * (flow + heating + fa[at, :])

        lateral(parts, finish)

    def solid_step(cur, nxt):
        for i in range(NP * PR // CHUNK):
            at = pl.ds(BASE + CHUNK * i, CHUNK)
            u = fu[cur, at, :]
            up, un = z_next(u), z_prev(u)
            slope = up - u
            k = fb[at, :] / (fa[at, :] + slope * slope)
            kp, kn = z_both(k, matrix)
            for j, (value, both) in enumerate(((u, up + un), (k, kp + kn), (k * u, kp * up + kn * un))):
                vz[2 * j, at, :] = value + 0.5 * both
                vz[2 * j + 1, at, :] = both
            vz[6, at, :] = k

        def parts(x, c):
            at = pl.multiple_of(row_of(x) + 8 * c, 8)
            found = []
            for j in range(3):
                whole = lambda r: vz[2 * j, pl.ds(r, 8), :]
                both = lambda r: vz[2 * j + 1, pl.ds(r, 8), :]
                found.append((whole(at - 1) + whole(at + 1) + both(at), both(at - 1) + both(at + 1)))
            return found

        def finish(x, c, sums):
            at = pl.ds(pl.multiple_of(row_of(x) + 8 * c, 8), 8)
            u, k = fu[cur, at, :], vz[6, at, :]
            top = ff[at, :] + k * sums[0] + sums[2]
            bottom = 16.0 * k + sums[1] + 6.0
            fu[nxt, at, :] = 0.2 * u + fm[at, :] * (top / bottom)

        lateral(parts, finish)

    @pl.loop(0, MACRO)
    def _(m):
        @pl.when(team == 0)
        def _():
            thermal_prepare()

            @pl.loop(0, SUBS // 2)
            def _(i):
                thermal_step(m * SUBS + 2 * i, 0, 1)
                thermal_step(m * SUBS + 2 * i + 1, 1, 0)

        @pl.when(team == 1)
        def _():
            solid_prepare()

            @pl.loop(0, SUBS // 2)
            def _(i):
                solid_step(0, 1)
                solid_step(1, 0)

        @pl.when(m == 0)
        def _():
            for x in range(BX):
                nb[x] = fu[0, pl.ds(row_of(x + H) + H, BY), :]
            send_block(nb, 1, 1, OWN1, PART1)
            forward(1, PART1)
            relay(OWN1)
            relay(PART1)
            receive_strips(OWN1, fu.at[0])
            unpack_partner(1)
            receive_strips(PART1, fl)

    for x in range(BX):
        out[0, x] = fu[0, pl.ds(row_of(x + H) + H, BY), :]

    for m in range(MACRO):
        for piece in range(3):
            body_copy(nb, m, piece).wait_send()
    for kind in range(KINDS):
        wait_sent(kind)


def local(state, coef, mask, src_brick, power):
    vmem = pl.BlockSpec(memory_space=pltpu.VMEM)
    hbm = pl.BlockSpec(memory_space=pltpu.HBM)
    flat = pltpu.VMEM((ROWS, NZ), jnp.float32)
    block = pltpu.VMEM((BX, BY, NZ), jnp.float32)
    return pl.pallas_call(
        kernel,
        name="fields",
        out_shape=jax.ShapeDtypeStruct((1, BX, BY, NZ), jnp.float32),
        in_specs=[hbm] * 5,
        out_specs=vmem,
        scratch_shapes=[
            pltpu.VMEM((2, ROWS, NZ), jnp.float32),
            flat, flat,
            pltpu.VMEM((7, ROWS, NZ), jnp.float32),
            flat, flat, flat,
            pltpu.VMEM((MACRO * SUBS, BX // BRICK + 2, PR, NZ), jnp.float32),
            block, block, block,
            pltpu.VMEM((BY * BX, NZ), jnp.float32),
            pltpu.VMEM((3, 2, BX * H, NZ), jnp.float32),
            pltpu.VMEM((2, BX, BY, NZ), jnp.float32),
            pltpu.VMEM((KINDS, 2, H, BY, NZ), jnp.float32),
            pltpu.VMEM((KINDS, 2, BX * H, NZ), jnp.float32),
            pltpu.VMEM((KINDS, 4, H * H, NZ), jnp.float32),
            pltpu.VMEM((BY, NZ // BRICK, BX), jnp.int32),
            pltpu.SMEM((MACRO * SUBS, NSRC), jnp.int32),
            pltpu.SMEM((MACRO * SUBS, NSRC), jnp.float32),
            pltpu.SemaphoreType.DMA((5,)),
            pltpu.SemaphoreType.DMA((2, 3)),
            pltpu.SemaphoreType.DMA((2, 3)),
            pltpu.SemaphoreType.DMA((KINDS, 8)),
            pltpu.SemaphoreType.DMA((KINDS, 8)),
        ],
        compiler_params=pltpu.CompilerParams(
            collective_id=0, has_side_effects=True, vmem_limit_bytes=60 * 2**20
        ),
    )(state, coef, jnp.transpose(mask, (1, 2, 0)), src_brick, power)


def solution(mesh):
    placed = (P("team", "gx", "gy", None), P("team", "gx", "gy", None), P("gx", "gy", None), P(), P())
    return jax.shard_map(
        local, mesh=mesh, in_specs=placed, out_specs=P("team", "gx", "gy", None), check_vma=False
    )
```

```python
import jax
import jax.numpy as jnp
from jax import lax
from jax.experimental import pallas as pl
from jax.experimental.pallas import tpu as pltpu
from jax.sharding import PartitionSpec as P

MESH = pl.DeviceIdType.MESH
BRICK = 8
MACRO = 2
SUBS = 4
NSRC = 16
H = 4
BX, BY, NZ = 32, 16, 128
PR = BY + 2 * H
NP = BX + 2 * H
BASE = 32
ROWS = BASE + NP * PR + 32
CHUNK = 192
DIRS = ((-1, 0), (1, 0), (0, -1), (0, 1), (-1, -1), (-1, 1), (1, -1), (1, 1))
KINDS = 5
OPP = tuple(DIRS.index((-dx, -dy)) for dx, dy in DIRS)
OWN0, BASE0, PART0, OWN1, PART1 = range(KINDS)

PIECES = ((0, H), (BX - H, H), (H, BX - 2 * H))


def row_of(xp):
    return BASE + PR * xp


def z_next(value):
    lane = lax.broadcasted_iota(jnp.int32, value.shape, 1)
    return jnp.where(lane == NZ - 1, 0.0, pltpu.roll(value, NZ - 1, 1))


def z_prev(value):
    lane = lax.broadcasted_iota(jnp.int32, value.shape, 1)
    return jnp.where(lane == 0, 0.0, pltpu.roll(value, 1, 1))


def shift_matrix():
    source = lax.broadcasted_iota(jnp.int32, (NZ, 2 * NZ), 0)
    target = lax.broadcasted_iota(jnp.int32, (NZ, 2 * NZ), 1)
    following = jnp.logical_and(target < NZ, source == target + 1)
    previous = jnp.logical_and(target >= NZ, source == target - NZ - 1)
    once = jnp.logical_or(following, previous).astype(jnp.bfloat16)
    return jnp.concatenate([once, once], axis=0)


def z_both(value, matrix):
    high = value.astype(jnp.bfloat16)
    rest = (value - high.astype(jnp.float32)).astype(jnp.bfloat16)
    both = jnp.dot(jnp.concatenate([high, rest], axis=1), matrix, preferred_element_type=jnp.float32)
    return both[:, :NZ], both[:, NZ:]


def kernel(
    state, coef, mask_in, bricks_in, powers_in, out,
    fu, fb, fl, vz, fa, ff, fm, src, sv, cv, nb, act, pk, pb, xland, yland, cland, mask, bricks, powers,
    local_sem, body_send, body_recv, send, recv,
):
    team, gx, gy = lax.axis_index("team"), lax.axis_index("gx"), lax.axis_index("gy")
    ngx, ngy = lax.axis_size("gx"), lax.axis_size("gy")
    partner = (1 - team, gx, gy)

    state_copy = pltpu.make_async_copy(state.at[0], sv, local_sem.at[0])
    coef_copy = pltpu.make_async_copy(coef.at[0], cv, local_sem.at[1])
    mask_copy = pltpu.make_async_copy(mask_in, mask, local_sem.at[2])
    brick_copy = pltpu.make_async_copy(bricks_in, bricks, local_sem.at[3])
    power_copy = pltpu.make_async_copy(powers_in, powers, local_sem.at[4])
    state_copy.start()
    coef_copy.start()
    mask_copy.start()
    brick_copy.start()
    power_copy.start()

    def exists(d):
        dx, dy = DIRS[d]
        ok = None
        for delta, pos, size in ((dx, gx, ngx), (dy, gy, ngy)):
            if delta:
                this = pos > 0 if delta < 0 else pos < size - 1
                ok = this if ok is None else jnp.logical_and(ok, this)
        return ok

    def near(d, crossed=False):
        return (1 - team if crossed else team, gx + DIRS[d][0], gy + DIRS[d][1])

    barrier = pltpu.get_barrier_semaphore()
    pl.semaphore_signal(barrier, inc=1, device_id=partner, device_id_type=MESH)
    count = jnp.int32(1)
    for d in range(4):
        @pl.when(exists(d))
        def _():
            pl.semaphore_signal(barrier, inc=1, device_id=near(d), device_id_type=MESH)
            if d >= 2:
                pl.semaphore_signal(barrier, inc=1, device_id=near(d, True), device_id_type=MESH)
        count = count + (2 if d >= 2 else 1) * exists(d).astype(jnp.int32)

    def body_copy(source, m, piece):
        first, planes = PIECES[piece]
        return pltpu.make_async_remote_copy(
            src_ref=source.at[pl.ds(first, planes)], dst_ref=pb.at[m, pl.ds(first, planes)],
            send_sem=body_send.at[m, piece], recv_sem=body_recv.at[m, piece],
            device_id=partner, device_id_type=MESH,
        )

    strips = {
        OWN0: (sv, pk.at[0], False),
        BASE0: (cv, pk.at[2], False),
        PART0: (pb.at[0], pk.at[0], True),
        OWN1: (nb, pk.at[1], False),
        PART1: (pb.at[1], pk.at[1], True),
    }
    ALONG_X, ALONG_Y = (0, 1), (2, 3)

    def strip(kind, d):
        block, packed, crossed = strips[kind]
        dx, dy = DIRS[d]
        if dy == 0:
            o = OPP[d]
            source = block.at[pl.ds(0 if dx < 0 else BX - H, H)]
            target = xland.at[kind, o]
        elif dx == 0:
            o = OPP[d]
            source = packed.at[d - 2]
            target = yland.at[kind, o - 2]
        else:
            o = DIRS.index((-dx, dy))
            source = yland.at[kind, 0 if dy < 0 else 1, pl.ds(0 if dx < 0 else (BX - H) * H, H * H)]
            target = cland.at[kind, o - 4]
        to = near(d, crossed) if dx == 0 else (team, gx + dx, gy)
        return pltpu.make_async_remote_copy(
            src_ref=source, dst_ref=target, send_sem=send.at[kind, d],
            recv_sem=recv.at[kind, o], device_id=to, device_id_type=MESH,
        )

    def start_strips(kind, ways):
        for d in ways:
            @pl.when(exists(d))
            def _():
                strip(kind, d).start()

    def landing(kind, d):
        return xland.at[kind, d] if d < 2 else yland.at[kind, d - 2] if d < 4 else cland.at[kind, d - 4]

    def arrived(kind, d):
        ref = landing(kind, d)
        pltpu.make_async_remote_copy(
            src_ref=ref, dst_ref=ref, send_sem=send.at[kind, d], recv_sem=recv.at[kind, d],
            device_id=near(d % 4), device_id_type=MESH,
        ).wait_recv()

    def relay(kind):
        for d in ALONG_Y:
            @pl.when(exists(d))
            def _():
                arrived(kind, d)
                for corner in range(4, 8):
                    if DIRS[corner][1] == DIRS[d][1]:
                        @pl.when(exists(corner))
                        def _():
                            strip(kind, corner).start()

    def receive_strips(kind, flat):
        for d in ALONG_Y + ALONG_X + (4, 5, 6, 7):
            dx, dy = DIRS[d]

            @pl.when(exists(d))
            def _():
                if d not in ALONG_Y:
                    arrived(kind, d)
                row = 0 if dy < 0 else PR - H
                first = 0 if dx < 0 else NP - H
                if dy == 0:
                    for j in range(H):
                        flat[pl.ds(row_of(first + j) + H, BY), :] = xland[kind, d, j]
                elif dx == 0:
                    for x in range(BX):
                        flat[pl.ds(row_of(x + H) + row, H), :] = yland[kind, d - 2, pl.ds(H * x, H), :]
                else:
                    for j in range(H):
                        flat[pl.ds(row_of(first + j) + row, H), :] = cland[kind, d - 4, pl.ds(H * j, H), :]

    def wait_sent(kind):
        for d in range(8):
            @pl.when(exists(d))
            def _():
                strip(kind, d).wait_send()

    def pack(slot, block):
        for x in range(BX):
            pk[slot, 0, pl.ds(H * x, H), :] = block[x, 0:H, :]
            pk[slot, 1, pl.ds(H * x, H), :] = block[x, BY - H:BY, :]

    def send_block(block, slot, m, own, other):
        body_copy(block, m, 0).start()
        body_copy(block, m, 1).start()
        pack(slot, block)
        start_strips(other, ALONG_Y)
        start_strips(own, ALONG_Y + ALONG_X)
        if m:
            body_copy(block, m, 2).start()

    def forward(m, kind):
        for side in range(2):
            body_copy(nb, m, side).wait_recv()
            start_strips(kind, (side,))

    def unpack_partner(m):
        body_copy(nb, m, 2).wait_recv()
        for x in range(BX):
            fl[pl.ds(row_of(x + H) + H, BY), :] = pb[m, x]

    state_copy.wait()
    pl.semaphore_wait(barrier, count)
    send_block(sv, 0, 0, OWN0, PART0)

    segment = lax.broadcasted_iota(jnp.int32, (NZ // BRICK, NZ), 0)
    spread = (lax.broadcasted_iota(jnp.int32, (NZ // BRICK, NZ), 1) // BRICK == segment).astype(jnp.float32)
    unit = jnp.where(team == 0, 1.0, 2.0)
    mask_copy.wait()
    for y in range(BY):
        lit = lax.dot_general(
            (mask[y] == 1).astype(jnp.float32), spread, (((0,), (0,)), ((), ())),
            preferred_element_type=jnp.float32,
        )
        act[pl.ds(y * BX, BX), :] = jnp.where(lit > 0.5, unit, 0.05 * unit)
    coef_copy.wait()
    for x in range(BX):
        cv[x] = cv[x] * act[pl.ds(x, BY, stride=BX), :]
    pack(2, cv)
    start_strips(BASE0, ALONG_Y + ALONG_X)
    body_copy(sv, 0, 2).start()

    zeros = jnp.zeros((64, NZ), jnp.float32)

    @pl.loop(0, ROWS // 64)
    def _(i):
        at = pl.ds(pl.multiple_of(i * 64, 64), 64)
        fu[0, at, :] = zeros
        fu[1, at, :] = zeros
        fb[at, :] = zeros
        fl[at, :] = zeros
        fm[at, :] = zeros

    guard = jnp.zeros((8, NZ), jnp.float32)
    for j in range(7):
        vz[j, pl.ds(BASE - 8, 8), :] = guard
        vz[j, pl.ds(row_of(NP), 8), :] = guard

    for x in range(BX):
        at = pl.ds(row_of(x + H) + H, BY)
        fu[0, at, :] = sv[x]
        fb[at, :] = cv[x]

    row = lax.broadcasted_iota(jnp.int32, (PR, NZ), 0)
    low = jnp.where(gy == 0, H, 0)
    high = jnp.where(gy == ngy - 1, PR - H, PR)
    factor = jnp.where(team == 0, 0.025, 0.8)
    inside = jnp.where(jnp.logical_and(row >= low, row < high), factor, 0.0)

    @pl.loop(jnp.where(gx == 0, H, 0), jnp.where(gx == ngx - 1, NP - H, NP))
    def _(xp):
        fm[pl.ds(pl.multiple_of(row_of(xp), 8), PR), :] = inside

    forward(0, PART0)
    brick_copy.wait()
    power_copy.wait()

    relay(OWN0)
    relay(PART0)

    nbz = NZ // BRICK
    nby = ngy * (BY // BRICK)

    @pl.when(team == 0)
    def _():
        lane_brick = lax.broadcasted_iota(jnp.int32, (PR, NZ), 1) // BRICK
        row_brick = gy * (BY // BRICK) + (row + BRICK - H) // BRICK - 1
        first_x = gx * (BX // BRICK) - 1

        @pl.loop(0, MACRO * SUBS)
        def _(g):
            acc = [jnp.zeros((PR, NZ), jnp.float32) for _ in range(BX // BRICK + 2)]
            for i in range(NSRC):
                b = bricks[g, i]
                p = 2.0 * powers[g, i]
                here = jnp.where(
                    jnp.logical_and(lane_brick == b % nbz, row_brick == (b // nbz) % nby), p, 0.0
                )
                bx = b // (nbz * nby) - first_x
                acc = [a + jnp.where(bx == j, here, 0.0) for j, a in enumerate(acc)]
            for j, a in enumerate(acc):
                src[g, j] = a

    relay(BASE0)
    receive_strips(OWN0, fu.at[0])
    receive_strips(BASE0, fb)
    unpack_partner(0)
    receive_strips(PART0, fl)

    matrix = shift_matrix()

    def thermal_prepare():
        for i in range(NP * PR // CHUNK):
            at = pl.ds(BASE + CHUNK * i, CHUNK)
            w = fl[at, :]
            slope = z_next(w) - w
            fa[at, :] = slope * slope

    def solid_prepare():
        for i in range(NP * PR // CHUNK):
            at = pl.ds(BASE + CHUNK * i, CHUNK)
            w = fl[at, :]
            fa[at, :] = 2.0 + 0.5 * w * w
            ff[at, :] = 6.0 * (z_next(w) - z_prev(w))

    def lateral(parts, finish, skip):
        @pl.loop(0, PR // 8)
        def _(c):
            window = [parts(x, c) for x in (skip - 1, skip)]
            for x in range(skip, NP - skip):
                window.append(parts(x + 1, c))
                below, here, above = window
                finish(x, c, [lo[0] + hi[0] + me[1] for lo, me, hi in zip(below, here, above)])
                window.pop(0)

    def thermal_step(g, cur, nxt):
        for i in range(NP * PR // CHUNK):
            at = pl.ds(BASE + CHUNK * i, CHUNK)
            t = fu[cur, at, :]
            tp, tn = z_next(t), z_prev(t)
            k = fb[at, :] * (1.0 + 0.5 * jnp.tanh(t))
            kp, kn = z_both(k, matrix)
            vz[0, at, :] = k
            vz[1, at, :] = k * t
            vz[2, at, :] = tp + tn
            vz[3, at, :] = kp + kn
            vz[4, at, :] = kp * tp + kn * tn

        def parts(x, c):
            at = pl.multiple_of(row_of(x) + 8 * c, 8)
            found = []
            for load, z in ((lambda r: fu[cur, pl.ds(r, 8), :], 2), (lambda r: vz[0, pl.ds(r, 8), :], 3),
                            (lambda r: vz[1, pl.ds(r, 8), :], 4)):
                found.append((load(at), load(at - 1) + load(at + 1) + vz[z, pl.ds(at, 8), :]))
            return found

        def finish(x, c, sums):
            at = pl.ds(pl.multiple_of(row_of(x) + 8 * c, 8), 8)
            t, k = fu[cur, at, :], vz[0, at, :]
            flow = k * sums[0] + sums[2] - t * (6.0 * k + sums[1])
            heating = src[g, (x + BRICK - H) // BRICK, pl.ds(pl.multiple_of(8 * c, 8), 8), :]
            fu[nxt, at, :] = t + fm[at, :] * (flow + heating + fa[at, :])

        lateral(parts, finish, 1 + cur)

    def solid_step(cur, nxt):
        for i in range(NP * PR // CHUNK):
            at = pl.ds(BASE + CHUNK * i, CHUNK)
            u = fu[cur, at, :]
            up, un = z_next(u), z_prev(u)
            slope = up - u
            k = fb[at, :] / (fa[at, :] + slope * slope)
            kp, kn = z_both(k, matrix)
            for j, (value, both) in enumerate(((u, up + un), (k, kp + kn), (k * u, kp * up + kn * un))):
                vz[2 * j, at, :] = value + 0.5 * both
                vz[2 * j + 1, at, :] = both
            vz[6, at, :] = k

        def parts(x, c):
            at = pl.multiple_of(row_of(x) + 8 * c, 8)
            found = []
            for j in range(3):
                whole = lambda r: vz[2 * j, pl.ds(r, 8), :]
                both = lambda r: vz[2 * j + 1, pl.ds(r, 8), :]
                found.append((whole(at - 1) + whole(at + 1) + both(at), both(at - 1) + both(at + 1)))
            return found

        def finish(x, c, sums):
            at = pl.ds(pl.multiple_of(row_of(x) + 8 * c, 8), 8)
            u, k = fu[cur, at, :], vz[6, at, :]
            top = ff[at, :] + k * sums[0] + sums[2]
            bottom = 16.0 * k + sums[1] + 6.0
            fu[nxt, at, :] = 0.2 * u + fm[at, :] * (top / bottom)

        lateral(parts, finish, 1 + cur)

    @pl.loop(0, MACRO)
    def _(m):
        @pl.when(team == 0)
        def _():
            thermal_prepare()

            @pl.loop(0, SUBS // 2)
            def _(i):
                thermal_step(m * SUBS + 2 * i, 0, 1)
                thermal_step(m * SUBS + 2 * i + 1, 1, 0)

        @pl.when(team == 1)
        def _():
            solid_prepare()

            @pl.loop(0, SUBS // 2)
            def _(i):
                solid_step(0, 1)
                solid_step(1, 0)

        @pl.when(m == 0)
        def _():
            for x in range(BX):
                nb[x] = fu[0, pl.ds(row_of(x + H) + H, BY), :]
            send_block(nb, 1, 1, OWN1, PART1)
            forward(1, PART1)
            relay(OWN1)
            relay(PART1)
            receive_strips(OWN1, fu.at[0])
            unpack_partner(1)
            receive_strips(PART1, fl)

    for x in range(BX):
        out[0, x] = fu[0, pl.ds(row_of(x + H) + H, BY), :]

    for m in range(MACRO):
        for piece in range(3):
            body_copy(nb, m, piece).wait_send()
    for kind in range(KINDS):
        wait_sent(kind)


def local(state, coef, mask, src_brick, power):
    vmem = pl.BlockSpec(memory_space=pltpu.VMEM)
    hbm = pl.BlockSpec(memory_space=pltpu.HBM)
    flat = pltpu.VMEM((ROWS, NZ), jnp.float32)
    block = pltpu.VMEM((BX, BY, NZ), jnp.float32)
    return pl.pallas_call(
        kernel,
        name="fields",
        out_shape=jax.ShapeDtypeStruct((1, BX, BY, NZ), jnp.float32),
        in_specs=[hbm] * 5,
        out_specs=vmem,
        scratch_shapes=[
            pltpu.VMEM((2, ROWS, NZ), jnp.float32),
            flat, flat,
            pltpu.VMEM((7, ROWS, NZ), jnp.float32),
            flat, flat, flat,
            pltpu.VMEM((MACRO * SUBS, BX // BRICK + 2, PR, NZ), jnp.float32),
            block, block, block,
            pltpu.VMEM((BY * BX, NZ), jnp.float32),
            pltpu.VMEM((3, 2, BX * H, NZ), jnp.float32),
            pltpu.VMEM((2, BX, BY, NZ), jnp.float32),
            pltpu.VMEM((KINDS, 2, H, BY, NZ), jnp.float32),
            pltpu.VMEM((KINDS, 2, BX * H, NZ), jnp.float32),
            pltpu.VMEM((KINDS, 4, H * H, NZ), jnp.float32),
            pltpu.VMEM((BY, NZ // BRICK, BX), jnp.int32),
            pltpu.SMEM((MACRO * SUBS, NSRC), jnp.int32),
            pltpu.SMEM((MACRO * SUBS, NSRC), jnp.float32),
            pltpu.SemaphoreType.DMA((5,)),
            pltpu.SemaphoreType.DMA((2, 3)),
            pltpu.SemaphoreType.DMA((2, 3)),
            pltpu.SemaphoreType.DMA((KINDS, 8)),
            pltpu.SemaphoreType.DMA((KINDS, 8)),
        ],
        compiler_params=pltpu.CompilerParams(
            collective_id=0, has_side_effects=True, vmem_limit_bytes=60 * 2**20
        ),
    )(state, coef, jnp.transpose(mask, (1, 2, 0)), src_brick, power)


def solution(mesh):
    placed = (P("team", "gx", "gy", None), P("team", "gx", "gy", None), P("gx", "gy", None), P(), P())
    return jax.shard_map(
        local, mesh=mesh, in_specs=placed, out_specs=P("team", "gx", "gy", None), check_vma=False
    )
```

```python
import jax
import jax.numpy as jnp
from jax import lax
from jax.experimental import pallas as pl
from jax.experimental.pallas import tpu as pltpu
from jax.sharding import PartitionSpec as P

MESH = pl.DeviceIdType.MESH
BRICK = 8
MACRO = 2
SUBS = 4
NSRC = 16
H = 4
BX, BY, NZ = 32, 16, 128
PR = BY + 2 * H
NP = BX + 2 * H
BASE = 32
ROWS = BASE + NP * PR + 32
CHUNK = 192
DIRS = ((-1, 0), (1, 0), (0, -1), (0, 1), (-1, -1), (-1, 1), (1, -1), (1, 1))
KINDS = 5
OPP = tuple(DIRS.index((-dx, -dy)) for dx, dy in DIRS)
OWN0, BASE0, PART0, OWN1, PART1 = range(KINDS)

PIECES = ((0, H), (BX - H, H), (H, BX - 2 * H))


def row_of(xp):
    return BASE + PR * xp


def z_next(value):
    lane = lax.broadcasted_iota(jnp.int32, value.shape, 1)
    return jnp.where(lane == NZ - 1, 0.0, pltpu.roll(value, NZ - 1, 1))


def z_prev(value):
    lane = lax.broadcasted_iota(jnp.int32, value.shape, 1)
    return jnp.where(lane == 0, 0.0, pltpu.roll(value, 1, 1))


def shift_matrix():
    source = lax.broadcasted_iota(jnp.int32, (NZ, 2 * NZ), 0)
    target = lax.broadcasted_iota(jnp.int32, (NZ, 2 * NZ), 1)
    following = jnp.logical_and(target < NZ, source == target + 1)
    previous = jnp.logical_and(target >= NZ, source == target - NZ - 1)
    once = jnp.logical_or(following, previous).astype(jnp.bfloat16)
    return jnp.concatenate([once, once], axis=0)


def z_both(value, matrix):
    high = value.astype(jnp.bfloat16)
    rest = (value - high.astype(jnp.float32)).astype(jnp.bfloat16)
    both = jnp.dot(jnp.concatenate([high, rest], axis=1), matrix, preferred_element_type=jnp.float32)
    return both[:, :NZ], both[:, NZ:]


def kernel(
    state, coef, mask_in, bricks_in, powers_in, out,
    fu, fb, fl, vz, fa, ff, fm, src, sv, cv, nb, act, pk, pb, xland, yland, cland, mask, bricks, powers,
    local_sem, body_send, body_recv, send, recv,
):
    team, gx, gy = lax.axis_index("team"), lax.axis_index("gx"), lax.axis_index("gy")
    ngx, ngy = lax.axis_size("gx"), lax.axis_size("gy")
    partner = (1 - team, gx, gy)

    state_copy = pltpu.make_async_copy(state.at[0], sv, local_sem.at[0])
    coef_copy = pltpu.make_async_copy(coef.at[0], cv, local_sem.at[1])
    mask_copy = pltpu.make_async_copy(mask_in, mask, local_sem.at[2])
    brick_copy = pltpu.make_async_copy(bricks_in, bricks, local_sem.at[3])
    power_copy = pltpu.make_async_copy(powers_in, powers, local_sem.at[4])
    state_copy.start()
    coef_copy.start()
    mask_copy.start()
    brick_copy.start()
    power_copy.start()

    def exists(d):
        dx, dy = DIRS[d]
        ok = None
        for delta, pos, size in ((dx, gx, ngx), (dy, gy, ngy)):
            if delta:
                this = pos > 0 if delta < 0 else pos < size - 1
                ok = this if ok is None else jnp.logical_and(ok, this)
        return ok

    def near(d, crossed=False):
        return (1 - team if crossed else team, gx + DIRS[d][0], gy + DIRS[d][1])

    barrier = pltpu.get_barrier_semaphore()
    pl.semaphore_signal(barrier, inc=1, device_id=partner, device_id_type=MESH)
    count = jnp.int32(1)
    for d in range(4):
        @pl.when(exists(d))
        def _():
            pl.semaphore_signal(barrier, inc=1, device_id=near(d), device_id_type=MESH)
            if d >= 2:
                pl.semaphore_signal(barrier, inc=1, device_id=near(d, True), device_id_type=MESH)
        count = count + (2 if d >= 2 else 1) * exists(d).astype(jnp.int32)

    def body_copy(source, m, piece):
        first, planes = PIECES[piece]
        return pltpu.make_async_remote_copy(
            src_ref=source.at[pl.ds(first, planes)], dst_ref=pb.at[m, pl.ds(first, planes)],
            send_sem=body_send.at[m, piece], recv_sem=body_recv.at[m, piece],
            device_id=partner, device_id_type=MESH,
        )

    strips = {
        OWN0: (sv, pk.at[0], False),
        BASE0: (cv, pk.at[2], False),
        PART0: (pb.at[0], pk.at[0], True),
        OWN1: (nb, pk.at[1], False),
        PART1: (pb.at[1], pk.at[1], True),
    }
    ALONG_X, ALONG_Y = (0, 1), (2, 3)

    def strip(kind, d):
        block, packed, crossed = strips[kind]
        dx, dy = DIRS[d]
        if dy == 0:
            o = OPP[d]
            source = block.at[pl.ds(0 if dx < 0 else BX - H, H)]
            target = xland.at[kind, o]
        elif dx == 0:
            o = OPP[d]
            source = packed.at[d - 2]
            target = yland.at[kind, o - 2]
        else:
            o = DIRS.index((-dx, dy))
            source = yland.at[kind, 0 if dy < 0 else 1, pl.ds(0 if dx < 0 else (BX - H) * H, H * H)]
            target = cland.at[kind, o - 4]
        to = near(d, crossed) if dx == 0 else (team, gx + dx, gy)
        return pltpu.make_async_remote_copy(
            src_ref=source, dst_ref=target, send_sem=send.at[kind, d],
            recv_sem=recv.at[kind, o], device_id=to, device_id_type=MESH,
        )

    def start_strips(kind, ways):
        for d in ways:
            @pl.when(exists(d))
            def _():
                strip(kind, d).start()

    def landing(kind, d):
        return xland.at[kind, d] if d < 2 else yland.at[kind, d - 2] if d < 4 else cland.at[kind, d - 4]

    def arrived(kind, d):
        ref = landing(kind, d)
        pltpu.make_async_remote_copy(
            src_ref=ref, dst_ref=ref, send_sem=send.at[kind, d], recv_sem=recv.at[kind, d],
            device_id=near(d % 4), device_id_type=MESH,
        ).wait_recv()

    def relay(kind):
        for d in ALONG_Y:
            @pl.when(exists(d))
            def _():
                arrived(kind, d)
                for corner in range(4, 8):
                    if DIRS[corner][1] == DIRS[d][1]:
                        @pl.when(exists(corner))
                        def _():
                            strip(kind, corner).start()

    def receive_strips(kind, flat):
        for d in ALONG_Y + ALONG_X + (4, 5, 6, 7):
            dx, dy = DIRS[d]

            @pl.when(exists(d))
            def _():
                if d not in ALONG_Y:
                    arrived(kind, d)
                row = 0 if dy < 0 else PR - H
                first = 0 if dx < 0 else NP - H
                if dy == 0:
                    for j in range(H):
                        flat[pl.ds(row_of(first + j) + H, BY), :] = xland[kind, d, j]
                elif dx == 0:
                    for x in range(BX):
                        flat[pl.ds(row_of(x + H) + row, H), :] = yland[kind, d - 2, pl.ds(H * x, H), :]
                else:
                    for j in range(H):
                        flat[pl.ds(row_of(first + j) + row, H), :] = cland[kind, d - 4, pl.ds(H * j, H), :]

    def wait_sent(kind):
        for d in range(8):
            @pl.when(exists(d))
            def _():
                strip(kind, d).wait_send()

    def pack(slot, load):
        for x in range(BX):
            pk[slot, 0, pl.ds(H * x, H), :] = load(x, 0)
            pk[slot, 1, pl.ds(H * x, H), :] = load(x, BY - H)

    def send_block(block, slot, m, own, other):
        body_copy(block, m, 0).start()
        body_copy(block, m, 1).start()
        start_strips(other, ALONG_Y)
        start_strips(own, ALONG_Y + ALONG_X)
        if m:
            body_copy(block, m, 2).start()

    def forward(m, kind):
        for side in range(2):
            body_copy(nb, m, side).wait_recv()
            start_strips(kind, (side,))

    def unpack_partner(m):
        body_copy(nb, m, 2).wait_recv()
        for x in range(BX):
            fl[pl.ds(row_of(x + H) + H, BY), :] = pb[m, x]

    state_copy.wait()
    pack(0, lambda x, y: sv[x, y:y + H, :])
    pl.semaphore_wait(barrier, count)
    send_block(sv, 0, 0, OWN0, PART0)

    segment = lax.broadcasted_iota(jnp.int32, (NZ // BRICK, NZ), 0)
    spread = (lax.broadcasted_iota(jnp.int32, (NZ // BRICK, NZ), 1) // BRICK == segment).astype(jnp.float32)
    unit = jnp.where(team == 0, 1.0, 2.0)
    mask_copy.wait()
    for y in range(BY):
        lit = lax.dot_general(
            (mask[y] == 1).astype(jnp.float32), spread, (((0,), (0,)), ((), ())),
            preferred_element_type=jnp.float32,
        )
        act[pl.ds(y * BX, BX), :] = jnp.where(lit > 0.5, unit, 0.05 * unit)
    coef_copy.wait()
    for x in range(BX):
        cv[x] = cv[x] * act[pl.ds(x, BY, stride=BX), :]
    pack(2, lambda x, y: cv[x, y:y + H, :])
    start_strips(BASE0, ALONG_Y + ALONG_X)
    body_copy(sv, 0, 2).start()

    zeros = jnp.zeros((64, NZ), jnp.float32)

    @pl.loop(0, ROWS // 64)
    def _(i):
        at = pl.ds(pl.multiple_of(i * 64, 64), 64)
        fu[0, at, :] = zeros
        fu[1, at, :] = zeros
        fb[at, :] = zeros
        fl[at, :] = zeros
        fm[at, :] = zeros

    guard = jnp.zeros((8, NZ), jnp.float32)
    for j in range(7):
        vz[j, pl.ds(BASE - 8, 8), :] = guard
        vz[j, pl.ds(row_of(NP), 8), :] = guard

    for x in range(BX):
        at = pl.ds(row_of(x + H) + H, BY)
        fu[0, at, :] = sv[x]
        fb[at, :] = cv[x]

    row = lax.broadcasted_iota(jnp.int32, (PR, NZ), 0)
    low = jnp.where(gy == 0, H, 0)
    high = jnp.where(gy == ngy - 1, PR - H, PR)
    factor = jnp.where(team == 0, 0.025, 0.8)
    inside = jnp.where(jnp.logical_and(row >= low, row < high), factor, 0.0)

    @pl.loop(jnp.where(gx == 0, H, 0), jnp.where(gx == ngx - 1, NP - H, NP))
    def _(xp):
        fm[pl.ds(pl.multiple_of(row_of(xp), 8), PR), :] = inside

    forward(0, PART0)
    brick_copy.wait()
    power_copy.wait()

    relay(OWN0)
    relay(PART0)

    nbz = NZ // BRICK
    nby = ngy * (BY // BRICK)

    @pl.when(team == 0)
    def _():
        lane_brick = lax.broadcasted_iota(jnp.int32, (PR, NZ), 1) // BRICK
        row_brick = gy * (BY // BRICK) + (row + BRICK - H) // BRICK - 1
        first_x = gx * (BX // BRICK) - 1

        @pl.loop(0, MACRO * SUBS)
        def _(g):
            acc = [jnp.zeros((PR, NZ), jnp.float32) for _ in range(BX // BRICK + 2)]
            for i in range(NSRC):
                b = bricks[g, i]
                p = 2.0 * powers[g, i]
                here = jnp.where(
                    jnp.logical_and(lane_brick == b % nbz, row_brick == (b // nbz) % nby), p, 0.0
                )
                bx = b // (nbz * nby) - first_x
                acc = [a + jnp.where(bx == j, here, 0.0) for j, a in enumerate(acc)]
            for j, a in enumerate(acc):
                src[g, j] = a

    relay(BASE0)
    receive_strips(OWN0, fu.at[0])
    receive_strips(BASE0, fb)
    receive_strips(PART0, fl)
    unpack_partner(0)

    matrix = shift_matrix()

    def thermal_prepare():
        for i in range(NP * PR // CHUNK):
            at = pl.ds(BASE + CHUNK * i, CHUNK)
            w = fl[at, :]
            slope = z_next(w) - w
            fa[at, :] = slope * slope

    def solid_prepare():
        for i in range(NP * PR // CHUNK):
            at = pl.ds(BASE + CHUNK * i, CHUNK)
            w = fl[at, :]
            fa[at, :] = 2.0 + 0.5 * w * w
            following, previous = z_both(w, matrix)
            ff[at, :] = 6.0 * (following - previous)

    def lateral(parts, finish, skip):
        @pl.loop(0, PR // 8)
        def _(c):
            window = [parts(x, c) for x in (skip - 1, skip)]
            for x in range(skip, NP - skip):
                window.append(parts(x + 1, c))
                below, here, above = window
                finish(x, c, [lo[0] + hi[0] + me[1] for lo, me, hi in zip(below, here, above)])
                window.pop(0)

    def thermal_step(g, cur, nxt):
        for i in range(NP * PR // CHUNK):
            at = pl.ds(BASE + CHUNK * i, CHUNK)
            t = fu[cur, at, :]
            tp, tn = z_next(t), z_prev(t)
            k = fb[at, :] * (1.0 + 0.5 * jnp.tanh(t))
            kp, kn = z_both(k, matrix)
            vz[0, at, :] = k
            vz[1, at, :] = k * t
            vz[2, at, :] = tp + tn
            vz[3, at, :] = kp + kn
            vz[4, at, :] = kp * tp + kn * tn

        def parts(x, c):
            at = pl.multiple_of(row_of(x) + 8 * c, 8)
            found = []
            for load, z in ((lambda r: fu[cur, pl.ds(r, 8), :], 2), (lambda r: vz[0, pl.ds(r, 8), :], 3),
                            (lambda r: vz[1, pl.ds(r, 8), :], 4)):
                found.append((load(at), load(at - 1) + load(at + 1) + vz[z, pl.ds(at, 8), :]))
            return found

        def finish(x, c, sums):
            at = pl.ds(pl.multiple_of(row_of(x) + 8 * c, 8), 8)
            t, k = fu[cur, at, :], vz[0, at, :]
            flow = k * sums[0] + sums[2] - t * (6.0 * k + sums[1])
            heating = src[g, (x + BRICK - H) // BRICK, pl.ds(pl.multiple_of(8 * c, 8), 8), :]
            fu[nxt, at, :] = t + fm[at, :] * (flow + heating + fa[at, :])

        lateral(parts, finish, 1 + cur)

    def solid_step(cur, nxt):
        for i in range(NP * PR // CHUNK):
            at = pl.ds(BASE + CHUNK * i, CHUNK)
            u = fu[cur, at, :]
            up, un = z_next(u), z_prev(u)
            slope = up - u
            k = fb[at, :] / (fa[at, :] + slope * slope)
            kp, kn = z_both(k, matrix)
            for j, (value, both) in enumerate(((u, up + un), (k, kp + kn), (k * u, kp * up + kn * un))):
                vz[2 * j, at, :] = value + 0.5 * both
                vz[2 * j + 1, at, :] = both
            vz[6, at, :] = k

        def parts(x, c):
            at = pl.multiple_of(row_of(x) + 8 * c, 8)
            found = []
            for j in range(3):
                whole = lambda r: vz[2 * j, pl.ds(r, 8), :]
                both = lambda r: vz[2 * j + 1, pl.ds(r, 8), :]
                found.append((whole(at - 1) + whole(at + 1) + both(at), both(at - 1) + both(at + 1)))
            return found

        def finish(x, c, sums):
            at = pl.ds(pl.multiple_of(row_of(x) + 8 * c, 8), 8)
            u, k = fu[cur, at, :], vz[6, at, :]
            top = ff[at, :] + k * sums[0] + sums[2]
            bottom = 16.0 * k + sums[1] + 6.0
            fu[nxt, at, :] = 0.2 * u + fm[at, :] * (top / bottom)

        lateral(parts, finish, 1 + cur)

    @pl.loop(0, MACRO)
    def _(m):
        @pl.when(team == 0)
        def _():
            thermal_prepare()

            @pl.loop(0, SUBS // 2)
            def _(i):
                thermal_step(m * SUBS + 2 * i, 0, 1)
                thermal_step(m * SUBS + 2 * i + 1, 1, 0)

        @pl.when(team == 1)
        def _():
            solid_prepare()

            @pl.loop(0, SUBS // 2)
            def _(i):
                solid_step(0, 1)
                solid_step(1, 0)

        @pl.when(m == 0)
        def _():
            pack(1, lambda x, y: fu[0, pl.ds(row_of(x + H) + H + y, H), :])
            for x in range(BX):
                nb[x] = fu[0, pl.ds(row_of(x + H) + H, BY), :]
            send_block(nb, 1, 1, OWN1, PART1)
            forward(1, PART1)
            relay(OWN1)
            relay(PART1)
            receive_strips(OWN1, fu.at[0])
            receive_strips(PART1, fl)
            unpack_partner(1)

    for x in range(BX):
        out[0, x] = fu[0, pl.ds(row_of(x + H) + H, BY), :]

    for m in range(MACRO):
        for piece in range(3):
            body_copy(nb, m, piece).wait_send()
    for kind in range(KINDS):
        wait_sent(kind)


def local(state, coef, mask, src_brick, power):
    vmem = pl.BlockSpec(memory_space=pltpu.VMEM)
    hbm = pl.BlockSpec(memory_space=pltpu.HBM)
    flat = pltpu.VMEM((ROWS, NZ), jnp.float32)
    block = pltpu.VMEM((BX, BY, NZ), jnp.float32)
    return pl.pallas_call(
        kernel,
        name="fields",
        out_shape=jax.ShapeDtypeStruct((1, BX, BY, NZ), jnp.float32),
        in_specs=[hbm] * 5,
        out_specs=vmem,
        scratch_shapes=[
            pltpu.VMEM((2, ROWS, NZ), jnp.float32),
            flat, flat,
            pltpu.VMEM((7, ROWS, NZ), jnp.float32),
            flat, flat, flat,
            pltpu.VMEM((MACRO * SUBS, BX // BRICK + 2, PR, NZ), jnp.float32),
            block, block, block,
            pltpu.VMEM((BY * BX, NZ), jnp.float32),
            pltpu.VMEM((3, 2, BX * H, NZ), jnp.float32),
            pltpu.VMEM((2, BX, BY, NZ), jnp.float32),
            pltpu.VMEM((KINDS, 2, H, BY, NZ), jnp.float32),
            pltpu.VMEM((KINDS, 2, BX * H, NZ), jnp.float32),
            pltpu.VMEM((KINDS, 4, H * H, NZ), jnp.float32),
            pltpu.VMEM((BY, NZ // BRICK, BX), jnp.int32),
            pltpu.SMEM((MACRO * SUBS, NSRC), jnp.int32),
            pltpu.SMEM((MACRO * SUBS, NSRC), jnp.float32),
            pltpu.SemaphoreType.DMA((5,)),
            pltpu.SemaphoreType.DMA((2, 3)),
            pltpu.SemaphoreType.DMA((2, 3)),
            pltpu.SemaphoreType.DMA((KINDS, 8)),
            pltpu.SemaphoreType.DMA((KINDS, 8)),
        ],
        compiler_params=pltpu.CompilerParams(
            collective_id=0, has_side_effects=True, vmem_limit_bytes=60 * 2**20
        ),
    )(state, coef, jnp.transpose(mask, (1, 2, 0)), src_brick, power)


def solution(mesh):
    placed = (P("team", "gx", "gy", None), P("team", "gx", "gy", None), P("gx", "gy", None), P(), P())
    return jax.shard_map(
        local, mesh=mesh, in_specs=placed, out_specs=P("team", "gx", "gy", None), check_vma=False
    )
```
